32 devices in a mesh: dp: 4 (over y, x), fsdp: 8 (over z, core).
Axes of the slice: x: 2, y: 2, z: 4, core: 2. Of those that a mesh axis runs over, the one named last changes fastest.
Arguments:
- tokens: bfloat16 [32, 1024, 768], P(('dp', 'fsdp')), may hold values from -6 to 6
- cotangent: bfloat16 [32, 1024, 768], P(('dp', 'fsdp')), may hold values from -6 to 6
- segments: int32 [32, 1024], P(('dp', 'fsdp')), may hold values from 0 to 7, never falling along the last dimension, each value on 1 to 512 neighbouring positions
- owners: int32 [12], replicated, may hold values from 0 to 31, as said below
- matrices: float32 [768, 9216], P(('dp', 'fsdp'))
- average: float32 [768, 9216], P(('dp', 'fsdp'))
- vectors: float32 [4, 768], P(None, ('dp', 'fsdp'))
- vec_moment: float32 [4, 768], P(None, ('dp', 'fsdp'))
- left_stats: float32 [32, 768, 768], P(('dp', 'fsdp')), as said below
- right_stats: float32 [32, 768, 768], P(('dp', 'fsdp')), as said below
- left_roots: float32 [32, 768, 768], P(('dp', 'fsdp'))
- right_roots: float32 [32, 768, 768], P(('dp', 'fsdp'))
Outputs:
- block_output: bfloat16 [32, 1024, 768], P(('dp', 'fsdp'))
- input_grad: bfloat16 [32, 1024, 768], P(('dp', 'fsdp'))
- matrix_grads: float32 [768, 9216], P(('dp', 'fsdp'))
- vector_grads: float32 [4, 768], P(None, ('dp', 'fsdp'))
- left_new: float32 [32, 768, 768], P(('dp', 'fsdp'))
- right_new: float32 [32, 768, 768], P(('dp', 'fsdp'))
- new_matrices: float32 [768, 9216], P(('dp', 'fsdp'))
- moment_new: float32 [4, 768], P(None, ('dp', 'fsdp'))
- vectors_new: float32 [4, 768], P(None, ('dp', 'fsdp'))
- average_new: float32 [768, 9216], P(('dp', 'fsdp'))
The draws below stay inside these ranges and needn't reach their ends.
Inputs may be any that keep to these rules, and one draw needn't show every extreme that they name: 12 distinct slot indices; the statistics of column block b are in slot owners[b]. `segments`: document ids never fall along a sequence; a document has at most 512 tokens. `left_stats`: each slot's matrix is symmetric. `right_stats`: each slot's matrix is symmetric.
All inputs are finite; a program needn't handle non-finite values.
Results may differ from the reference program's by a relative error of at most 0.012.
Values may be sent and summed in bfloat16 or wider, within the bound.
No kernel may reach another device: no remote copies, remote signals or barrier semaphores. Data moves between devices by JAX's collectives and lax.ppermute only.
A program may use at most 320 MiB of HBM per device.

```python
import math
import jax
import jax.numpy as jnp
import numpy as np
from jax import lax

D = 768
H = 12
HD = 64
FF = 3072
SEQ = 1024
DOCS = 8
BRANCHES = 48
MOST = 512
NBLK = 12
SLOTS = 32
ROWS = 32
TOKENS_ALL = 32768


def owner_table(key):
    inner = jax.random.permutation(key, SLOTS - 2) + 1
    fixed_ends = jnp.array([0, SLOTS - 1], dtype=jnp.int32)
    picks = jnp.concatenate([fixed_ends, inner[:NBLK - 2].astype(jnp.int32)])
    order = jax.random.permutation(jax.random.fold_in(key, 7), NBLK)
    return picks[order]


def draw_owners(key, part):
    return owner_table(jax.random.fold_in(key, 11))


def grad_scales():
    index = jnp.arange(NBLK)
    fc_end = 4 + FF // D
    root_d = math.sqrt(D)
    per_block = jnp.where(index < 3, 0.04 * root_d, jnp.where(index == 3, 0.06, jnp.where(index < fc_end, 0.018 * root_d, 0.094)))
    return per_block * math.sqrt(TOKENS_ALL)


def slot_strength(key):
    owners = owner_table(jax.random.fold_in(key, 11))
    scales = grad_scales()
    hits = (owners[None, :] == jnp.arange(SLOTS)[:, None]).astype(jnp.float32)
    owned = jnp.sum(hits, axis=1)
    picked = jnp.sum(hits * scales[None, :], axis=1)
    chosen = jnp.where(owned > 0.5, picked, scales[2])
    return D * chosen * chosen


def symmetric_matrix(key, strength, low_diag, high_diag):
    key_diag, key_off = jax.random.split(key)
    diag = jnp.exp(jax.random.uniform(key_diag, (SLOTS, D), minval=math.log(low_diag), maxval=math.log(high_diag)))
    raw = jnp.clip(jax.random.normal(key_off, (SLOTS, D, D)), -5.0, 5.0)
    mirrored = (raw + jnp.swapaxes(raw, 1, 2)) * math.sqrt(0.5)
    eye = jnp.eye(D, dtype=jnp.float32)
    matrix = mirrored * (1.0 / math.sqrt(D)) * (1.0 - eye) + eye * diag[:, :, None]
    return matrix * strength[:, None, None]


def draw_left_stats(key, part):
    return symmetric_matrix(jax.random.fold_in(key, 21), slot_strength(key), 1.0, 4.0)


def draw_right_stats(key, part):
    return symmetric_matrix(jax.random.fold_in(key, 22), slot_strength(key), 1.0, 4.0)


def draw_left_roots(key, part):
    return symmetric_matrix(jax.random.fold_in(key, 23), jnp.ones((SLOTS,), jnp.float32), 0.5, 2.0)


def draw_right_roots(key, part):
    return symmetric_matrix(jax.random.fold_in(key, 24), jnp.ones((SLOTS,), jnp.float32), 0.5, 2.0)


def block_spread():
    index = jnp.arange(NBLK)
    fc_end = 4 + FF // D
    small = 1.0 / math.sqrt(D)
    return jnp.where(index < 3, small, jnp.where(index == 3, 0.5, jnp.where(index < fc_end, small, 0.25)))


def weight_like(key):
    spread = jnp.repeat(block_spread(), D)
    raw = jnp.clip(jax.random.normal(key, (D, NBLK * D)), -4.0, 4.0)
    return raw * spread[None, :]


def draw_matrices(key, part):
    return weight_like(jax.random.fold_in(key, 31))


def draw_average(key, part):
    return weight_like(jax.random.fold_in(key, 32))


def draw_vectors(key, part):
    inner = jax.random.fold_in(key, 41)
    raw = jnp.clip(jax.random.normal(inner, (4, D)), -4.0, 4.0)
    kind = jnp.array([1.0, 0.0, 1.0, 0.0], jnp.float32)[:, None]
    return kind * (1.0 + 0.1 * raw) + (1.0 - kind) * 0.3 * raw


def draw_vec_moment(key, part):
    inner = jax.random.fold_in(key, 42)
    root_t = math.sqrt(TOKENS_ALL)
    first_branch_output = 0.07 * math.sqrt(D) * root_t
    second_branch_output = 0.018 * math.sqrt(FF) * root_t
    per_row = jnp.array([first_branch_output, first_branch_output, second_branch_output, second_branch_output], jnp.float32)
    factor = jnp.exp(jax.random.uniform(inner, (4, D), minval=0.0, maxval=math.log(4.0)))
    return per_row[:, None] * per_row[:, None] * factor


def level_of(stream_key, extent, cuts, smallest, high):
    loudness = 1.0
    for position, parts in cuts:
        draws = jax.random.uniform(jax.random.fold_in(jax.random.fold_in(stream_key, 6), position), (parts,), jnp.float32, smallest / len(cuts), high / len(cuts))
        loudness = loudness * jnp.repeat(jnp.exp(draws), extent[position] // parts).reshape((-1,) + (1,) * (len(extent) - 1 - position))
    return loudness


def profile(number_of, total, most, lean):
    weights = [(1 << 20) // math.isqrt(standing ** lean) + 1 for standing in range(2, number_of + 1)]
    surplus, given = total - most - (number_of - 1), [1] * (number_of - 1)
    while surplus > 0:
        free = [i for i in range(number_of - 1) if given[i] < most]
        whole, remaining = sum([weights[i] for i in free]), surplus
        for i in free:
            addition = min(most - given[i], max(1, remaining * weights[i] // whole), surplus)
            given[i] = given[i] + addition
            surplus = surplus - addition
    return np.array([most] + given)


def ragged(rng, count, total, most, lean):
    if count == 2:
        one = jax.random.randint(rng, (), max(1, total - most), min(most, total - 1) + 1)
        return jnp.stack([one, total - one])
    lengths = jnp.asarray(profile(count, total, most, lean), jnp.int32)
    couples = (count - 1) // 2
    giver, receiver = lengths[1:1 + 2 * couples:2], lengths[2:2 + 2 * couples:2]
    slack = jnp.minimum(giver - 1, most - receiver)
    passed = jax.random.randint(jax.random.fold_in(rng, 1), (couples,), 0, 1 << 20) % (slack + 1)
    lengths = lengths.at[1:1 + 2 * couples:2].set(giver - passed).at[2:2 + 2 * couples:2].set(receiver + passed)
    return lengths[jax.random.permutation(jax.random.fold_in(rng, 2), count)]


def normal_values(rng, shape, scale, bound, shards=(), kind=jnp.bfloat16):
    result = scale * jax.random.normal(rng, shape, jnp.float32)
    if shards:
        result = result * level_of(rng, shape, shards, -0.22, 0.18)
    return jnp.clip(result, -bound, bound).astype(kind)


def setup_inputs(seed: int = 0) -> dict:
    splits = jax.random.split(jax.random.key(seed), 13)
    return {
        "tokens": normal_values(splits[0], (ROWS, SEQ, D), 1.0, 6.0, ((0, 32),)),
        "cotangent": normal_values(splits[1], (ROWS, SEQ, D), 1.0, 6.0, ((0, 32),)),
        "segments": jax.vmap(lambda own: jnp.searchsorted(jnp.cumsum(ragged(own, DOCS, SEQ, MOST, 2)), jnp.arange(SEQ), side="right"))(jax.random.split(splits[2], ROWS)).reshape((ROWS, SEQ)).astype(jnp.int32),
        "owners": draw_owners(jax.random.fold_in(splits[12], 71), 0),
        "matrices": draw_matrices(jax.random.fold_in(splits[12], 71), 0),
        "average": draw_average(jax.random.fold_in(splits[12], 71), 0),
        "vectors": draw_vectors(jax.random.fold_in(splits[12], 71), 0),
        "vec_moment": draw_vec_moment(jax.random.fold_in(splits[12], 71), 0),
        "left_stats": draw_left_stats(jax.random.fold_in(splits[12], 71), 0),
        "right_stats": draw_right_stats(jax.random.fold_in(splits[12], 71), 0),
        "left_roots": draw_left_roots(jax.random.fold_in(splits[12], 71), 0),
        "right_roots": draw_right_roots(jax.random.fold_in(splits[12], 71), 0),
    }


@jax.custom_vjp
def low(v):
    return lax.optimization_barrier(v.astype(jnp.bfloat16)).astype(jnp.float32)

@jax.custom_vjp
def low_back(v):
    return v

def low_keep(v):
    return (low(v), None)

def low_pass(kept, grad):
    return (grad,)

def back_keep(v):
    return (v, None)

def back_low(kept, grad):
    return (low(grad),)
low.defvjp(low_keep, low_pass)
low_back.defvjp(back_keep, back_low)
HIGHEST = lax.Precision.HIGHEST

def hdot(left, right):
    return jnp.dot(left, right, precision=HIGHEST, preferred_element_type=jnp.float32)

def layer_norm(rows, norm_gain, shift):
    centre = rows - lax.optimization_barrier(jnp.mean(rows, axis=-1, keepdims=True))
    inverse_deviation = lax.rsqrt(lax.optimization_barrier(jnp.mean(centre * centre, axis=-1, keepdims=True)) + 1e-05)
    return centre * inverse_deviation * norm_gain + shift

def attend(queries, keys, values, segs):
    group, length = segs.shape
    width = min(512, length)
    count = length // width
    q_heads = queries.reshape(group, length, H, HD)
    k_heads = keys.reshape(group, length, H, HD)
    v_heads = values.reshape(group, length, H, HD)
    key_pos = jnp.arange(length, dtype=jnp.int32)

    def one_block(index):
        start = index * width
        q_block = lax.dynamic_slice_in_dim(q_heads, start, width, 1)
        seg_query = lax.dynamic_slice_in_dim(segs, start, width, 1)
        query_pos = start + jnp.arange(width, dtype=jnp.int32)
        allowed = (seg_query[:, :, None] == segs[:, None, :]) & (key_pos[None, None, :] <= query_pos[None, :, None])
        scores = low_back(jnp.einsum('gqhd,gkhd->ghqk', q_block, k_heads, precision=HIGHEST))
        scores = jnp.where(allowed[:, None], scores, -1e+30)
        top = lax.optimization_barrier(jnp.max(scores, axis=-1, keepdims=True))
        expo = jnp.exp(scores - top)
        probs = low(expo / lax.optimization_barrier(jnp.sum(expo, axis=-1, keepdims=True)))
        return jnp.einsum('ghqk,gkhd->gqhd', probs, v_heads, precision=HIGHEST)
    blocks = lax.map(jax.checkpoint(one_block), jnp.arange(count, dtype=jnp.int32))
    return jnp.moveaxis(blocks, 0, 1).reshape(group * length, H * HD)

def forward(block_inputs, mats, vecs, segs):
    weights = low(mats)
    params = low(vecs)
    w_qkv = weights[:, :3 * D]
    w_out = weights[:, 3 * D:4 * D]
    w_fc = weights[:, 4 * D:4 * D + FF]
    w_proj = weights[:, 4 * D + FF:]
    branch = BRANCHES ** (-0.5)
    rows = block_inputs.reshape(-1, D)
    first_branch_output = low(layer_norm(rows, params[0], params[1]))
    qkv = low_back(hdot(first_branch_output, w_qkv))
    queries = low(qkv[:, :D] * HD ** (-0.5))
    keys = low(qkv[:, D:2 * D])
    values = low(qkv[:, 2 * D:])
    mixed = low(low_back(attend(queries, keys, values, segs)))
    branch_one = low_back(hdot(mixed, w_out))
    middle_residual = rows + branch_one * branch
    second_branch_output = low(layer_norm(middle_residual, params[2], params[3]))
    hidden = low_back(hdot(second_branch_output, w_fc))
    active = low(jax.nn.gelu(hidden, approximate=True))
    branch_two = low_back(hdot(active, w_proj.T))
    return middle_residual + branch_two * branch

def pick_group():
    limit = max(1, 4096 // SEQ)
    best = 1
    for size in range(1, min(limit, ROWS) + 1):
        if ROWS % size == 0:
            best = size
    return best

def block_rates():
    index = jnp.arange(NBLK, dtype=jnp.int32)
    fc_end = 4 + FF // D
    small = 0.8 / math.sqrt(D)
    return jnp.where(index < 3, small, jnp.where(index == 3, 0.4, jnp.where(index < fc_end, small, 0.2)))

def reference(tokens, cotangent, segments, owners, matrices, average, vectors, vec_moment, left_stats, right_stats, left_roots, right_roots):
    group = pick_group()
    count = ROWS // group
    block_inputs = tokens.astype(jnp.float32).reshape(count, group, SEQ, D)
    cots = cotangent.astype(jnp.float32).reshape(count, group * SEQ, D)
    segs = segments.reshape(count, group, SEQ)

    def one_group(carry, item):
        mat_sum, vec_sum = carry
        x_group, c_group, s_group = item
        out, pull = jax.vjp(lambda xx, mm, vv: forward(xx, mm, vv, s_group), x_group, matrices, vectors)
        grad_x, grad_m, grad_v = pull(c_group)
        return ((mat_sum + grad_m, vec_sum + grad_v), (out, grad_x))
    start = (jnp.zeros((D, NBLK * D), jnp.float32), jnp.zeros((4, D), jnp.float32))
    (matrix_grads, vector_grads), (outs, grads) = lax.scan(one_group, start, (block_inputs, cots, segs))
    block_output = outs.reshape(ROWS, SEQ, D).astype(jnp.bfloat16)
    input_grad = grads.reshape(ROWS, SEQ, D).astype(jnp.bfloat16)
    grad_blocks = matrix_grads.reshape(D, NBLK, D)
    rates = block_rates()
    left_new = 0.5 * left_stats
    right_new = 0.5 * right_stats
    steps = []
    for index in range(NBLK):
        slot = owners[index]
        block = grad_blocks[:, index, :]
        left_new = left_new.at[slot].add(0.5 * hdot(block, block.T))
        right_new = right_new.at[slot].add(0.5 * hdot(block.T, block))
        precond = hdot(hdot(left_roots[slot], block), right_roots[slot])
        steps.append(precond * (rates[index] / jnp.sqrt(jnp.mean(precond * precond) + 1e-06)))
    step = jnp.stack(steps, axis=1).reshape(D, NBLK * D)
    new_matrices = matrices - step
    average_new = 0.9 * average + 0.1 * new_matrices
    moment_new = 0.5 * vec_moment + 0.5 * vector_grads * vector_grads
    vectors_new = vectors - 0.2 * vector_grads / (jnp.sqrt(moment_new) + 1e-08)
    return (block_output, input_grad, matrix_grads, vector_grads, left_new, right_new, new_matrices, moment_new, vectors_new, average_new)
```

```python
import functools
import math

import jax
import jax.numpy as jnp
from jax import lax
from jax.experimental import pallas as pl
from jax.experimental.pallas import tpu as pltpu
from jax.sharding import PartitionSpec as P

D = 768
H = 12
HD = 64
FF = 3072
BRANCHES = 48
MOST = 512
T = 256
NEG = -1e30
AXES = ("dp", "fsdp")
MIB = 1 << 20


def apply_layer_norm(rows):
    centre = rows - jnp.mean(rows, axis=-1, keepdims=True)
    inverse_deviation = lax.rsqrt(jnp.mean(centre * centre, axis=-1, keepdims=True) + 1e-05)
    return (centre * inverse_deviation, inverse_deviation)


def norm_backward_rule(gradient_output_rows, centered_input, inverse_deviation, norm_gain):
    depth_scaled_output = gradient_output_rows * norm_gain
    return inverse_deviation * (
        depth_scaled_output
        - jnp.mean(depth_scaled_output, axis=-1, keepdims=True)
        - centered_input * jnp.mean(depth_scaled_output * centered_input, axis=-1, keepdims=True)
    )


def contract_rows(left, right):
    return lax.dot_general(
        left, right, (((0,), (0,)), ((), ())), preferred_element_type=jnp.float32
    )


def contract_cols(left, right):
    return lax.dot_general(
        left, right, (((1,), (1,)), ((), ())), preferred_element_type=jnp.float32
    )


def gelu_tanh(value):
    return jax.nn.gelu(value, approximate=True)


def nt(a,b): return lax.dot_general(a,b,(((1,),(1,)),((),())),preferred_element_type=jnp.float32)
def nn(a,b): return lax.dot_general(a,b,(((1,),(0,)),((),())),preferred_element_type=jnp.float32)
def tn(a,b): return lax.dot_general(a,b,(((0,),(0,)),((),())),preferred_element_type=jnp.float32)

def fill_bias(segc_ref, segr_ref, bias, nq, most):
    for i in range(nq):
        for d in range(most+1):
            j=i-most+d
            if j<0: continue
            same = segc_ref[j*T:(j+1)*T,:] == segr_ref[:, i*T:(i+1)*T]
            if j==i:
                kp=lax.broadcasted_iota(jnp.int32,(T,T),0); qp=lax.broadcasted_iota(jnp.int32,(T,T),1)
                same = same & (kp<=qp)
            bias[i, d*T:(d+1)*T, :] = jnp.where(same,0.0,NEG)

def fwd_kernel(first_ref, q_ref,k_ref,v_ref,segc_ref,segr_ref,o_ref,lse_ref,bias,kh,vt,*,nq,most):
    @pl.when(pl.program_id(0)==0)
    def _(): fill_bias(segc_ref,segr_ref,bias,nq,most)
    lane=lax.broadcasted_iota(jnp.int32,(1,2*HD),1)
    kh[0]=jnp.where(lane<HD,k_ref[...],0)
    kh[1]=jnp.where(lane>=HD,k_ref[...],0)
    vt[...]=v_ref[...].T
    for i in range(nq):
        hi=(i+1)*T
        qt=q_ref[i*T:hi,:]
        def variant(n):
            lo=hi-n*T
            outs=[]
            for h in range(2):
                s=nt(kh[h,lo:hi,:],qt)+bias[i,(most+1-n)*T:,:]
                top=jnp.max(s,axis=0,keepdims=True)
                e=jnp.exp(s-top)
                tot=jnp.sum(e,axis=0,keepdims=True)
                ot=nn(vt[h*HD:(h+1)*HD,lo:hi],e.astype(jnp.bfloat16))
                outs.append(ot*(1.0/tot))
                lse_ref[0,h:h+1,i*T:hi]=top+jnp.log(tot)
            o_ref[i*T:hi,:]=jnp.concatenate(outs,axis=0).T.astype(jnp.bfloat16)
        for n in range(1,min(i,most)+2):
            pl.when(first_ref[i]==n)(functools.partial(variant,n))

def tiles_needed(seg, nq, most):
    last=seg[T-1::T]; first=seg[0::T]
    j=jnp.arange(nq)
    need=(last[None,:]>=first[:,None])&(j[None,:]<=j[:,None])
    return jnp.sum(need,axis=1).astype(jnp.int32)

def attend_fwd(qkv, seg, most=2):
    S=qkv.shape[0]; nq=S//T
    most=min(most,nq-1)
    first=tiles_needed(seg,nq,most)
    f=pl.pallas_call(functools.partial(fwd_kernel,nq=nq,most=most),
      grid_spec=pltpu.PrefetchScalarGridSpec(num_scalar_prefetch=1,grid=(H//2,),
       in_specs=[pl.BlockSpec((S,2*HD),lambda h,f:(0,h)),pl.BlockSpec((S,2*HD),lambda h,f:(0,H//2+h)),pl.BlockSpec((S,2*HD),lambda h,f:(0,H+h)),
                 pl.BlockSpec((S,1),lambda h,f:(0,0)),pl.BlockSpec((1,S),lambda h,f:(0,0))],
       out_specs=[pl.BlockSpec((S,2*HD),lambda h,f:(0,h)),pl.BlockSpec((1,2,S),lambda h,f:(h,0,0))],
       scratch_shapes=[pltpu.VMEM((nq,(most+1)*T,T),jnp.float32),pltpu.VMEM((2,S,2*HD),jnp.bfloat16),pltpu.VMEM((2*HD,S),jnp.bfloat16)]),
      out_shape=[jax.ShapeDtypeStruct((S,D),jnp.bfloat16),jax.ShapeDtypeStruct((H//2,2,S),jnp.float32)],
      compiler_params=pltpu.CompilerParams(vmem_limit_bytes=48<<20),name="attention_forward")
    return f(first,qkv,qkv,qkv,seg.reshape(S,1),seg.reshape(1,S))

def bwd_kernel(first_ref,q_ref,k_ref,v_ref,do_ref,lse_ref,segc_ref,segr_ref,g_ref,bias,kh,kt,dk,dv,*,nq,most,scale):
    @pl.when(pl.program_id(0)==0)
    def _(): fill_bias(segc_ref,segr_ref,bias,nq,most)
    lane=lax.broadcasted_iota(jnp.int32,(1,2*HD),1)
    kh[0]=jnp.where(lane<HD,k_ref[...],0)
    kh[1]=jnp.where(lane>=HD,k_ref[...],0)
    kt[...]=k_ref[...].T
    dk[...]=jnp.zeros_like(dk); dv[...]=jnp.zeros_like(dv)
    for i in range(nq):
        hi=(i+1)*T
        qt=q_ref[i*T:hi,:]; dot_=do_ref[i*T:hi,:]
        def variant(n):
            lo=hi-n*T
            outs=[]
            for h in range(2):
                mine=(lane<HD) if h==0 else (lane>=HD)
                qh=jnp.where(mine,qt,0); dh=jnp.where(mine,dot_,0)
                s=nt(kh[h,lo:hi,:],qt)+bias[i,(most+1-n)*T:,:]
                p=jnp.exp(s-lse_ref[0,h:h+1,i*T:hi])
                dp=nt(v_ref[lo:hi,:],dh)
                dv[lo:hi,:]+=nn(p.astype(jnp.bfloat16),dh)
                t=p*dp
                delta=jnp.sum(t,axis=0,keepdims=True)
                ds=(t-p*delta).astype(jnp.bfloat16)
                dk[lo:hi,:]+=nn(ds,qh)
                outs.append(nn(kt[h*HD:(h+1)*HD,lo:hi],ds))
            g_ref[0,i*T:hi,:]=(jnp.concatenate(outs,axis=0)*scale).T.astype(jnp.bfloat16)
        for n in range(1,min(i,most)+2):
            pl.when(first_ref[i]==n)(functools.partial(variant,n))
    g_ref[1]=dk[...].astype(jnp.bfloat16)
    g_ref[2]=dv[...].astype(jnp.bfloat16)

def attend_bwd(qkv, do, lse, seg, most=2):
    S=qkv.shape[0]; nq=S//T
    most=min(most,nq-1)
    first=tiles_needed(seg,nq,most)
    f=pl.pallas_call(functools.partial(bwd_kernel,nq=nq,most=most,scale=HD**-0.5),
      grid_spec=pltpu.PrefetchScalarGridSpec(num_scalar_prefetch=1,grid=(H//2,),
       in_specs=[pl.BlockSpec((S,2*HD),lambda h,f:(0,h)),pl.BlockSpec((S,2*HD),lambda h,f:(0,H//2+h)),pl.BlockSpec((S,2*HD),lambda h,f:(0,H+h)),
                 pl.BlockSpec((S,2*HD),lambda h,f:(0,h)),pl.BlockSpec((1,2,S),lambda h,f:(h,0,0)),
                 pl.BlockSpec((S,1),lambda h,f:(0,0)),pl.BlockSpec((1,S),lambda h,f:(0,0))],
       out_specs=pl.BlockSpec((3,S,2*HD),lambda h,f:(0,0,h)),
       scratch_shapes=[pltpu.VMEM((nq,(most+1)*T,T),jnp.float32),pltpu.VMEM((2,S,2*HD),jnp.bfloat16),pltpu.VMEM((2*HD,S),jnp.bfloat16),
          pltpu.VMEM((S,2*HD),jnp.float32),pltpu.VMEM((S,2*HD),jnp.float32)]),
      out_shape=jax.ShapeDtypeStruct((3,S,D),jnp.bfloat16),
      compiler_params=pltpu.CompilerParams(vmem_limit_bytes=48<<20),name="attention_backward")
    return f(first,qkv,qkv,qkv,do,lse,seg.reshape(S,1),seg.reshape(1,S))

def bit_groups(devices_dp, devices_fsdp):
    return devices_fsdp // 2, devices_dp


def xor_permute(value, mask, devices):
    return lax.ppermute(value, AXES, [(i, i ^ mask) for i in range(devices)])


def by_coordinate(pieces, coordinate, axis):
    count = len(pieces)
    shape = list(pieces[0].shape)
    shape.insert(axis, count)
    index = lax.broadcasted_iota(jnp.int32, tuple(shape), axis) ^ coordinate
    out = jnp.expand_dims(pieces[0], axis)
    for m in range(1, count):
        out = jnp.where(index == m, jnp.expand_dims(pieces[m], axis), out)
    return out


def dp_parts(dp):
    inner = 1 << ((dp.bit_length() - 1) // 2)
    return dp // inner, inner


def gather_halves(first, second, dp, fsdp):
    devices = dp * fsdp
    outer, inner = dp_parts(dp)
    chips = fsdp // 2
    rank = lax.axis_index(AXES)
    core, z = rank % 2, rank // 2 % chips
    x, y = rank // fsdp % inner, rank // (fsdp * inner)

    def spread(value, unit, count, coordinate, axis):
        pieces = [value] + [xor_permute(value, m * unit, devices) for m in range(1, count)]
        return by_coordinate(pieces, coordinate, axis)

    first = spread(first, 2, chips, z, 0)
    second = spread(second, 2, chips, z, 0)
    first = spread(first, fsdp, inner, x, 0)
    second = spread(second, fsdp * inner, outer, y, 0)
    first = spread(first, fsdp * inner, outer, y, 0)
    second = spread(second, fsdp, inner, x, 1)
    first = spread(first, 1, 2, core, 3)
    second = spread(second, 1, 2, core, 3)
    return first.reshape(-1, first.shape[-1]), second.reshape(-1, second.shape[-1])


def scatter_halves(whole, cut, dp, fsdp):
    devices = dp * fsdp
    outer, inner = dp_parts(dp)
    chips = fsdp // 2
    rank = lax.axis_index(AXES)
    core, z = rank % 2, rank // 2 % chips
    x, y = rank // fsdp % inner, rank // (fsdp * inner)

    def fold(value, unit, count, coordinate, axis, kind=jnp.bfloat16):
        take = lambda index: lax.dynamic_index_in_dim(value, index, axis, keepdims=False)
        total = take(coordinate).astype(jnp.float32)
        for m in range(1, count):
            got = xor_permute(take(coordinate ^ m), m * unit, devices)
            total = total + got.astype(jnp.float32)
        return total.astype(kind)

    value = whole.reshape(outer, inner, chips, 2, -1, whole.shape[-1])
    value = fold(value, 1, 2, core, 3)
    first, second = value[..., :cut], value[..., cut:]
    first = fold(first, fsdp, inner, x, 1)
    second = fold(second, fsdp * inner, outer, y, 0)
    first = fold(first, fsdp * inner, outer, y, 0)
    second = fold(second, fsdp, inner, x, 0)
    first = fold(first, 2, chips, z, 0, jnp.float32)
    second = fold(second, 2, chips, z, 0, jnp.float32)
    return first, second


def pack_kernel(owners_ref, grads_ref, out_ref):
    out_ref[...] = jnp.zeros_like(out_ref)
    for block in range(grads_ref.shape[1] // D):
        out_ref[owners_ref[block]] = grads_ref[:, block * D : (block + 1) * D]


def pack_blocks(owners, grads, devices):
    rows = grads.shape[0]
    return pl.pallas_call(
        pack_kernel,
        in_specs=[pl.BlockSpec(memory_space=pltpu.SMEM), pl.BlockSpec(memory_space=pltpu.VMEM)],
        out_specs=pl.BlockSpec(memory_space=pltpu.VMEM),
        out_shape=jax.ShapeDtypeStruct((devices, rows, D), jnp.bfloat16),
        name="pack_blocks",
    )(owners, grads)


def step_kernel(rate_ref, grad_ref, left_ref, right_ref, out_ref):
    half = nn(left_ref[...].astype(jnp.bfloat16), grad_ref[...]).astype(jnp.bfloat16)
    precond = nn(half, right_ref[...].astype(jnp.bfloat16))
    mean = jnp.sum(jnp.sum(precond * precond, axis=0, keepdims=True), axis=1, keepdims=True) * (
        1.0 / (D * D)
    )
    out_ref[...] = (precond * (rate_ref[0] * lax.rsqrt(mean + 1e-06))).astype(jnp.bfloat16)


def owner_step(rate, grad, left, right):
    vmem = pl.BlockSpec(memory_space=pltpu.VMEM)
    return pl.pallas_call(
        step_kernel,
        in_specs=[pl.BlockSpec(memory_space=pltpu.SMEM), vmem, vmem, vmem],
        out_specs=vmem,
        out_shape=jax.ShapeDtypeStruct((D, D), jnp.bfloat16),
        compiler_params=pltpu.CompilerParams(vmem_limit_bytes=32 * MIB),
        name="owner_step",
    )(rate.reshape(1), grad, left, right)


def update_kernel(owners_ref, step_ref, weight_ref, average_ref, new_ref, mean_ref):
    for block in range(weight_ref.shape[1] // D):
        columns = slice(block * D, (block + 1) * D)
        fresh = weight_ref[:, columns] - step_ref[owners_ref[block]].astype(jnp.float32)
        new_ref[:, columns] = fresh
        mean_ref[:, columns] = 0.9 * average_ref[:, columns] + 0.1 * fresh


def update_weights(owners, steps, weights, average):
    vmem = pl.BlockSpec(memory_space=pltpu.VMEM)
    return pl.pallas_call(
        update_kernel,
        in_specs=[pl.BlockSpec(memory_space=pltpu.SMEM), vmem, vmem, vmem],
        out_specs=[vmem, vmem],
        out_shape=[jax.ShapeDtypeStruct(weights.shape, jnp.float32)] * 2,
        compiler_params=pltpu.CompilerParams(vmem_limit_bytes=32 * MIB),
        name="update_weights",
    )(owners, steps, weights, average)


def block_rates(count):
    index = jnp.arange(count, dtype=jnp.int32)
    fc_end = 4 + FF // D
    small = 0.8 / math.sqrt(D)
    return jnp.where(
        index < 3, small, jnp.where(index == 3, 0.4, jnp.where(index < fc_end, small, 0.2))
    )


def on_device(
    dp,
    fsdp,
    tokens,
    cotangent,
    segments,
    owners,
    matrices,
    average,
    vectors,
    vec_moment,
    left_stats,
    right_stats,
    left_roots,
    right_roots,
):
    branch = BRANCHES ** (-0.5)
    scale = HD ** (-0.5)
    devices = dp * fsdp
    rank = lax.axis_index(AXES)
    rows_dev = matrices.shape[0]
    seg = segments[0]
    narrow = matrices.astype(jnp.bfloat16)
    vec_rows = jnp.pad(vectors.astype(jnp.bfloat16).T, ((0, 0), (0, 124)))
    cut = 1152
    early_a, early_b = gather_halves(
        jnp.concatenate([vec_rows, narrow[:, :cut]], axis=1), narrow[:, cut : 3 * D], dp, fsdp
    )
    rest = lax.all_gather(narrow[:, 3 * D :], AXES, axis=0, tiled=True)
    params = early_a[:, :4].T.astype(jnp.float32)
    w_qkv = jnp.concatenate([early_a[:, 128:], early_b], axis=1)
    w_out, w_fc, w_proj = rest[:, :D], rest[:, D : D + FF], rest[:, D + FF :]
    gain1, shift1, gain2, shift2 = params[0], params[1], params[2], params[3]
    block_inputs = tokens.reshape(-1, D).astype(jnp.float32)
    xhat1, r1 = apply_layer_norm(block_inputs)
    a1 = (xhat1 * gain1 + shift1).astype(jnp.bfloat16)
    qkv = jnp.dot(a1, w_qkv, preferred_element_type=jnp.float32)
    factor = jnp.where(jnp.arange(3 * D) < D, scale, 1.0).astype(jnp.float32)
    qkv = (qkv * factor).astype(jnp.bfloat16)
    mixed, sums = attend_fwd(qkv, seg)
    x1 = block_inputs + jnp.dot(mixed, w_out, preferred_element_type=jnp.float32) * branch
    xhat2, r2 = apply_layer_norm(x1)
    a2 = (xhat2 * gain2 + shift2).astype(jnp.bfloat16)
    hidden = jnp.dot(a2, w_fc, preferred_element_type=jnp.float32)
    active_f, gelu_pull = jax.vjp(gelu_tanh, hidden)
    active = active_f.astype(jnp.bfloat16)
    outputs = x1 + contract_cols(active, w_proj) * branch
    block_output = outputs.reshape(tokens.shape).astype(jnp.bfloat16)
    dy = cotangent.reshape(-1, D).astype(jnp.float32)
    dz2 = (dy * branch).astype(jnp.bfloat16)
    grad_proj = contract_rows(dz2, active)
    dm = jnp.dot(dz2, w_proj, preferred_element_type=jnp.float32)
    du = gelu_pull(dm)[0].astype(jnp.bfloat16)
    grad_fc = contract_rows(a2, du)
    dh2 = contract_cols(du, w_fc)
    dx1 = dy + norm_backward_rule(dh2, xhat2, r2, gain2)
    dz = (dx1 * branch).astype(jnp.bfloat16)
    grad_out = contract_rows(mixed, dz)
    early_terms = jnp.concatenate(
        [grad_out.astype(jnp.bfloat16), grad_fc.astype(jnp.bfloat16), grad_proj.astype(jnp.bfloat16)], axis=1
    )
    early_grads = lax.psum_scatter(early_terms, AXES, scatter_dimension=0, tiled=True)
    do = contract_cols(dz, w_out).astype(jnp.bfloat16)
    dqkv = attend_bwd(qkv, do, sums, seg)
    grad_qkv = [contract_rows(a1, dqkv[t]).astype(jnp.bfloat16) for t in range(3)]
    dh1 = sum(contract_cols(dqkv[t], w_qkv[:, t * D : (t + 1) * D]) for t in range(3))
    input_rows = dx1 + norm_backward_rule(dh1, xhat1, r1, gain1)
    input_grad = input_rows.reshape(tokens.shape).astype(jnp.bfloat16)
    vector_terms = jnp.stack(
        [
            jnp.sum(dh1 * xhat1, axis=0),
            jnp.sum(dh1, axis=0),
            jnp.sum(dh2 * xhat2, axis=0),
            jnp.sum(dh2, axis=0),
        ],
        axis=1,
    )
    vector_terms = jnp.pad(vector_terms.astype(jnp.bfloat16), ((0, 0), (0, 124)))
    late_a, late_b = scatter_halves(
        jnp.concatenate([vector_terms] + grad_qkv, axis=1), 128 + cut, dp, fsdp
    )
    vector_grads = late_a[:, :4].T
    matrix_grads = jnp.concatenate([late_a[:, 128:], late_b, early_grads.astype(jnp.float32)], axis=1)
    outgoing = pack_blocks(owners, matrix_grads.astype(jnp.bfloat16), devices)
    whole = lax.all_to_all(outgoing, AXES, split_axis=0, concat_axis=0, tiled=True)
    block_grad = whole.reshape(D, D)
    mine = (owners == rank).astype(jnp.float32)
    rate = jnp.sum(mine * block_rates(owners.shape[0]))
    step = owner_step(rate, block_grad, left_roots[0], right_roots[0])
    returned = lax.all_to_all(
        step.reshape(devices, rows_dev, D), AXES, split_axis=0, concat_axis=0, tiled=True
    )
    left_next = 0.5 * left_stats[0] + 0.5 * contract_cols(block_grad, block_grad)
    right_next = 0.5 * right_stats[0] + 0.5 * contract_rows(block_grad, block_grad)
    new_matrices, average_new = update_weights(owners, returned, matrices, average)
    moment_new = 0.5 * vec_moment + 0.5 * vector_grads * vector_grads
    vectors_new = vectors - 0.2 * vector_grads / (jnp.sqrt(moment_new) + 1e-08)
    return (
        block_output,
        input_grad,
        matrix_grads,
        vector_grads,
        left_next[None],
        right_next[None],
        new_matrices,
        moment_new,
        vectors_new,
        average_new,
    )


def solution(mesh):
    in_specs = (
        P(("dp", "fsdp"), None, None),
        P(("dp", "fsdp"), None, None),
        P(("dp", "fsdp"), None),
        P(),
        P(("dp", "fsdp"), None),
        P(("dp", "fsdp"), None),
        P(None, ("dp", "fsdp")),
        P(None, ("dp", "fsdp")),
        P(("dp", "fsdp"), None, None),
        P(("dp", "fsdp"), None, None),
        P(("dp", "fsdp"), None, None),
        P(("dp", "fsdp"), None, None),
    )
    out_specs = (
        P(("dp", "fsdp"), None, None),
        P(("dp", "fsdp"), None, None),
        P(("dp", "fsdp"), None),
        P(None, ("dp", "fsdp")),
        P(("dp", "fsdp"), None, None),
        P(("dp", "fsdp"), None, None),
        P(("dp", "fsdp"), None),
        P(None, ("dp", "fsdp")),
        P(None, ("dp", "fsdp")),
        P(("dp", "fsdp"), None),
    )
    return jax.shard_map(
        functools.partial(on_device, mesh.shape["dp"], mesh.shape["fsdp"]), mesh=mesh, in_specs=in_specs, out_specs=out_specs, check_vma=False
    )
```

```python
import functools
import math

import jax
import jax.numpy as jnp
from jax import lax
from jax.experimental import pallas as pl
from jax.experimental.pallas import tpu as pltpu
from jax.sharding import PartitionSpec as P

D = 768
H = 12
HD = 64
FF = 3072
BRANCHES = 48
BRANCH = BRANCHES ** (-0.5)
SCALE = HD ** (-0.5)
MOST = 512
T = 256
LEAD = 256
EXT = LEAD + 3 * D
HALF = EXT // 2
CHUNK = 768
NEG = -1e30
GELU_A = math.sqrt(2.0 / math.pi)
GELU_B = 0.044715
AXES = ("dp", "fsdp")
MIB = 1 << 20
SMALL = pl.CostEstimate(flops=1024, bytes_accessed=1024, transcendentals=0)


def nt(a, b):
    return lax.dot_general(a, b, (((1,), (1,)), ((), ())), preferred_element_type=jnp.float32)


def nn(a, b):
    return lax.dot_general(a, b, (((1,), (0,)), ((), ())), preferred_element_type=jnp.float32)


def tn(a, b):
    return lax.dot_general(a, b, (((0,), (0,)), ((), ())), preferred_element_type=jnp.float32)


def row_norm(rows):
    centre = rows - jnp.mean(rows, axis=-1, keepdims=True)
    inverse = lax.rsqrt(jnp.mean(centre * centre, axis=-1, keepdims=True) + 1e-05)
    return centre * inverse, inverse


def norm_backward(gradient, xhat, inverse, gain):
    e = gradient * gain
    return inverse * (
        e - jnp.mean(e, axis=-1, keepdims=True) - xhat * jnp.mean(e * xhat, axis=-1, keepdims=True)
    )


def row_sums(gradient, xhat):
    return jnp.concatenate(
        [jnp.sum(gradient * xhat, axis=0, keepdims=True), jnp.sum(gradient, axis=0, keepdims=True)],
        axis=0,
    )


def whole_spec(shape, **kwargs):
    return pl.BlockSpec(shape, lambda *_: (0,) * len(shape), **kwargs)


ONCE = dict(pipeline_mode=pl.Buffered(1))
SCALARS = pl.BlockSpec(memory_space=pltpu.SMEM)


def params_of(vmem):
    return pltpu.CompilerParams(vmem_limit_bytes=vmem * MIB)


def qkv_kernel(core_ref, tokens_ref, own_ref, other_ref, qkv_ref, normed_ref, params_ref):
    core = core_ref[0]

    @pl.when(pl.program_id(0) == 0)
    def _():
        lead = jnp.where(core == 0, own_ref[:, :128].astype(jnp.float32), other_ref[:, :128].astype(jnp.float32))
        params_ref[...] = lead.T[:8]

    xhat, _ = row_norm(tokens_ref[...].astype(jnp.float32))
    normed = (xhat * params_ref[0:1] + params_ref[1:2]).astype(jnp.bfloat16)
    normed_ref[...] = normed.T
    for side, weights in ((core, own_ref), (1 - core, other_ref)):
        columns = pl.ds(pl.multiple_of(side * HALF, 128), HALF)
        qkv_ref[:, columns] = nn(normed, weights[...]).astype(jnp.bfloat16)


def qkv_forward(core, tokens, own, other):
    length = tokens.shape[0]
    return pl.pallas_call(
        qkv_kernel,
        grid=(length // T,),
        in_specs=[
            SCALARS,
            pl.BlockSpec((T, D), lambda i: (i, 0)),
            whole_spec((D, HALF), **ONCE),
            whole_spec((D, HALF), **ONCE),
        ],
        out_specs=[
            pl.BlockSpec((T, EXT), lambda i: (i, 0)),
            pl.BlockSpec((D, T), lambda i: (0, i)),
            whole_spec((8, D)),
        ],
        out_shape=[
            jax.ShapeDtypeStruct((length, EXT), jnp.bfloat16),
            jax.ShapeDtypeStruct((D, length), jnp.bfloat16),
            jax.ShapeDtypeStruct((8, D), jnp.float32),
        ],
        compiler_params=params_of(32),
        cost_estimate=SMALL,
        name="qkv_forward",
    )(core, tokens, own, other)


def split_rows(total, buffer, core, rows, keep_ref, send_ref):
    for part in range(total.shape[0] // rows):
        place = part // 2 * rows
        buffer[part % 2, place : place + rows] = total[part * rows : (part + 1) * rows]
    keep_ref[...] = buffer[core].astype(jnp.bfloat16)
    send_ref[...] = buffer[1 - core].astype(jnp.bfloat16)


def forward_kernel(
    rows_dev, core_ref, mixed_ref, tokens_ref, cotangent_ref, weights_ref, params_ref,
    output_ref, residual_ref, slope_ref, keep_ref, send_ref,
    active, incoming, buffer,
):
    step = pl.program_id(0)
    tiles = active.shape[0]
    parts = FF // CHUNK

    @pl.when(step < tiles)
    def _():
        weights = lambda block: weights_ref[:, block * D : (block + 1) * D]
        residual = tokens_ref[...].astype(jnp.float32) + nn(mixed_ref[...], weights(0)) * BRANCH
        residual_ref[...] = residual
        xhat, _ = row_norm(residual)
        normed = (xhat * params_ref[2:3] + params_ref[3:4]).astype(jnp.bfloat16)
        scaled = (cotangent_ref[...].astype(jnp.float32) * BRANCH).astype(jnp.bfloat16)
        incoming[step] = scaled.T
        total = residual
        for chunk in range(parts):
            columns = slice(chunk * CHUNK, (chunk + 1) * CHUNK)
            u = nn(normed, weights(1 + chunk))
            square = u * u
            bend = jnp.tanh(u * (GELU_A + (GELU_A * GELU_B) * square))
            half = 0.5 + 0.5 * bend
            product = u * half
            hidden = product.astype(jnp.bfloat16)
            active[step, :, columns] = hidden
            slope = half + product * ((1.0 - bend) * (GELU_A + (3.0 * GELU_A * GELU_B) * square))
            slope_ref[:, columns] = slope.astype(jnp.bfloat16)
            total += nt(hidden, weights(1 + parts + chunk)) * BRANCH
        output_ref[...] = total.astype(jnp.bfloat16)

    for chunk in range(parts):
        @pl.when(step == tiles + chunk)
        def _(columns=slice(chunk * CHUNK, (chunk + 1) * CHUNK)):
            total = nn(incoming[0], active[0, :, columns])
            for tile in range(1, tiles):
                total += nn(incoming[tile], active[tile, :, columns])
            split_rows(total, buffer, core_ref[0], rows_dev, keep_ref, send_ref)


def block_forward(core, mixed, tokens, cotangent, weights, params, rows_dev):
    length = tokens.shape[0]
    tiles = length // T
    rows = lambda width: pl.BlockSpec((T, width), lambda i: (jnp.minimum(i, tiles - 1), 0))
    half = pl.BlockSpec((D // 2, CHUNK), lambda i: (0, jnp.maximum(i - tiles, 0)))
    return pl.pallas_call(
        functools.partial(forward_kernel, rows_dev),
        grid=(tiles + FF // CHUNK,),
        in_specs=[
            SCALARS, rows(D), rows(D), rows(D), whole_spec(weights.shape, **ONCE), whole_spec((8, D)),
        ],
        out_specs=[rows(D), rows(D), rows(FF), half, half],
        out_shape=[
            jax.ShapeDtypeStruct((length, D), jnp.bfloat16),
            jax.ShapeDtypeStruct((length, D), jnp.float32),
            jax.ShapeDtypeStruct((length, FF), jnp.bfloat16),
            jax.ShapeDtypeStruct((D // 2, FF), jnp.bfloat16),
            jax.ShapeDtypeStruct((D // 2, FF), jnp.bfloat16),
        ],
        scratch_shapes=[
            pltpu.VMEM((tiles, T, FF), jnp.bfloat16),
            pltpu.VMEM((tiles, D, T), jnp.bfloat16),
            pltpu.VMEM((2, D // 2, CHUNK), jnp.float32),
        ],
        compiler_params=params_of(52),
        cost_estimate=SMALL,
        name="block_forward",
    )(core, mixed, tokens, cotangent, weights, params)


def backward_kernel(
    rows_dev, core_ref, mixed_ref, residual_ref, cotangent_ref, slope_ref, weights_ref, params_ref,
    dx_ref, do_ref, sums_ref, keep_ref, send_ref, inner, normed_t, mixed_t, outer, buffer,
):
    step = pl.program_id(0)
    tiles = inner.shape[0]
    parts = FF // CHUNK

    @pl.when(step < tiles)
    def _():
        weights = lambda block: weights_ref[:, block * D : (block + 1) * D]
        xhat, inverse = row_norm(residual_ref[...])
        normed_t[step] = (xhat * params_ref[2:3] + params_ref[3:4]).astype(jnp.bfloat16).T
        mixed_t[step] = mixed_ref[...].T
        dy = cotangent_ref[...].astype(jnp.float32)
        scaled = (dy * BRANCH).astype(jnp.bfloat16)
        dh = jnp.zeros((T, D), jnp.float32)
        for chunk in range(parts):
            columns = slice(chunk * CHUNK, (chunk + 1) * CHUNK)
            slope = slope_ref[:, columns].astype(jnp.float32)
            du = (nn(scaled, weights(1 + parts + chunk)) * slope).astype(jnp.bfloat16)
            inner[step, :, columns] = du
            dh += nt(du, weights(1 + chunk))
        both = row_sums(dh, xhat)
        sums_ref[...] = jnp.where(step == 0, both, sums_ref[...] + both)
        dx = dy + norm_backward(dh, xhat, inverse, params_ref[2:3])
        dx_ref[...] = dx
        dz = (dx * BRANCH).astype(jnp.bfloat16)
        outer[step] = dz
        do_ref[...] = nt(dz, weights(0)).astype(jnp.bfloat16)

    def gradient(left, right, columns):
        total = nn(left[0], right[0, :, columns])
        for tile in range(1, tiles):
            total += nn(left[tile], right[tile, :, columns])
        split_rows(total, buffer, core_ref[0], rows_dev, keep_ref, send_ref)

    pl.when(step == tiles)(functools.partial(gradient, mixed_t, outer, slice(0, D)))
    for chunk in range(parts):
        columns = slice(chunk * CHUNK, (chunk + 1) * CHUNK)
        pl.when(step == tiles + 1 + chunk)(functools.partial(gradient, normed_t, inner, columns))


def block_backward(core, mixed, residual, cotangent, slope, weights, params, rows_dev):
    length = residual.shape[0]
    tiles = length // T
    rows = lambda width: pl.BlockSpec((T, width), lambda i: (jnp.minimum(i, tiles - 1), 0))
    half = pl.BlockSpec((D // 2, CHUNK), lambda i: (0, jnp.maximum(i - tiles, 0)))
    return pl.pallas_call(
        functools.partial(backward_kernel, rows_dev),
        grid=(tiles + 1 + FF // CHUNK,),
        in_specs=[
            SCALARS, rows(D), rows(D), rows(D), rows(FF), whole_spec(weights.shape, **ONCE),
            whole_spec((8, D)),
        ],
        out_specs=[rows(D), rows(D), whole_spec((2, D)), half, half],
        out_shape=[
            jax.ShapeDtypeStruct((length, D), jnp.float32),
            jax.ShapeDtypeStruct((length, D), jnp.bfloat16),
            jax.ShapeDtypeStruct((2, D), jnp.float32),
            jax.ShapeDtypeStruct((D // 2, D + FF), jnp.bfloat16),
            jax.ShapeDtypeStruct((D // 2, D + FF), jnp.bfloat16),
        ],
        scratch_shapes=[
            pltpu.VMEM((tiles, T, FF), jnp.bfloat16),
            pltpu.VMEM((tiles, D, T), jnp.bfloat16),
            pltpu.VMEM((tiles, D, T), jnp.bfloat16),
            pltpu.VMEM((tiles, T, D), jnp.bfloat16),
            pltpu.VMEM((2, D // 2, CHUNK), jnp.float32),
        ],
        compiler_params=params_of(52),
        cost_estimate=SMALL,
        name="block_backward",
    )(core, mixed, residual, cotangent, slope, weights, params)


def qkv_grad_kernel(rows_dev, core_ref, normed_ref, dqkv_ref, keep_ref, send_ref, buffer):
    split_rows(nn(normed_ref[...], dqkv_ref[0]), buffer, core_ref[0], rows_dev, keep_ref, send_ref)


def qkv_gradients(core, normed_t, dqkv, rows_dev):
    length = normed_t.shape[1]
    half = pl.BlockSpec((D // 2, D), lambda t: (0, t))
    return pl.pallas_call(
        functools.partial(qkv_grad_kernel, rows_dev),
        grid=(3,),
        in_specs=[
            SCALARS, whole_spec((D, length), **ONCE), pl.BlockSpec((1, length, D), lambda t: (t, 0, 0)),
        ],
        out_specs=[half, half],
        out_shape=[jax.ShapeDtypeStruct((D // 2, 3 * D), jnp.bfloat16)] * 2,
        scratch_shapes=[pltpu.VMEM((2, D // 2, D), jnp.float32)],
        compiler_params=params_of(40),
        cost_estimate=SMALL,
        name="qkv_gradients",
    )(core, normed_t, dqkv)


def input_kernel(
    core_ref, tokens_ref, dx_ref, dqkv_ref, own_ref, other_ref, params_ref,
    out_ref, sums_ref, wide,
):
    core = core_ref[0]
    wide[:, :LEAD] = jnp.zeros((T, LEAD), jnp.bfloat16)
    for t in range(3):
        wide[:, LEAD + t * D : LEAD + (t + 1) * D] = dqkv_ref[t]
    place = lambda side: pl.ds(pl.multiple_of(side * HALF, 128), HALF)
    dh = nt(wide[:, place(core)], own_ref[...]) + nt(wide[:, place(1 - core)], other_ref[...])
    xhat, inverse = row_norm(tokens_ref[...].astype(jnp.float32))
    both = row_sums(dh, xhat)
    sums_ref[...] = jnp.where(pl.program_id(0) == 0, both, sums_ref[...] + both)
    out_ref[...] = (dx_ref[...] + norm_backward(dh, xhat, inverse, params_ref[0:1])).astype(jnp.bfloat16)


def input_gradient(core, tokens, dx, dqkv, own, other, params):
    length = tokens.shape[0]
    rows = pl.BlockSpec((T, D), lambda i: (i, 0))
    return pl.pallas_call(
        input_kernel,
        grid=(length // T,),
        in_specs=[
            SCALARS, rows, rows, pl.BlockSpec((3, T, D), lambda i: (0, i, 0)),
            whole_spec((D, HALF), **ONCE), whole_spec((D, HALF), **ONCE), whole_spec((8, D)),
        ],
        out_specs=[rows, whole_spec((2, D))],
        out_shape=[
            jax.ShapeDtypeStruct((length, D), jnp.bfloat16),
            jax.ShapeDtypeStruct((2, D), jnp.float32),
        ],
        scratch_shapes=[pltpu.VMEM((T, EXT), jnp.bfloat16)],
        compiler_params=params_of(32),
        cost_estimate=SMALL,
        name="input_gradient",
    )(core, tokens, dx, dqkv, own, other, params)


def fill_bias(segc_ref, segr_ref, bias, nq, most):
    for i in range(nq):
        for d in range(most+1):
            j=i-most+d
            if j<0: continue
            same = segc_ref[j*T:(j+1)*T,:] == segr_ref[:, i*T:(i+1)*T]
            if j==i:
                kp=lax.broadcasted_iota(jnp.int32,(T,T),0); qp=lax.broadcasted_iota(jnp.int32,(T,T),1)
                same = same & (kp<=qp)
            bias[i, d*T:(d+1)*T, :] = jnp.where(same,0.0,NEG)

def fwd_kernel(first_ref, q_ref,k_ref,v_ref,segc_ref,segr_ref,o_ref,lse_ref,bias,kh,vt,*,nq,most):
    @pl.when(pl.program_id(0)==0)
    def _(): fill_bias(segc_ref,segr_ref,bias,nq,most)
    lane=lax.broadcasted_iota(jnp.int32,(1,2*HD),1)
    kh[0]=jnp.where(lane<HD,k_ref[...],0)
    kh[1]=jnp.where(lane>=HD,k_ref[...],0)
    vt[...]=v_ref[...].T
    for i in range(nq):
        hi=(i+1)*T
        qt=q_ref[i*T:hi,:]*SCALE
        def variant(n):
            lo=hi-n*T
            outs=[]
            for h in range(2):
                s=nt(kh[h,lo:hi,:],qt)+bias[i,(most+1-n)*T:,:]
                top=jnp.max(s,axis=0,keepdims=True)
                e=jnp.exp(s-top)
                tot=jnp.sum(e,axis=0,keepdims=True)
                ot=nn(vt[h*HD:(h+1)*HD,lo:hi],e.astype(jnp.bfloat16))
                outs.append(ot*(1.0/tot))
                lse_ref[0,h:h+1,i*T:hi]=top+jnp.log(tot)
            o_ref[i*T:hi,:]=jnp.concatenate(outs,axis=0).T.astype(jnp.bfloat16)
        for n in range(1,min(i,most)+2):
            pl.when(first_ref[i]==n)(functools.partial(variant,n))

def tiles_needed(seg, nq, most):
    last=seg[T-1::T]; first=seg[0::T]
    j=jnp.arange(nq)
    need=(last[None,:]>=first[:,None])&(j[None,:]<=j[:,None])
    return jnp.sum(need,axis=1).astype(jnp.int32)

def attend_fwd(qkv, seg, most=MOST//T):
    S=qkv.shape[0]; nq=S//T
    most=min(most,nq-1)
    first=tiles_needed(seg,nq,most)
    f=pl.pallas_call(functools.partial(fwd_kernel,nq=nq,most=most),
      grid_spec=pltpu.PrefetchScalarGridSpec(num_scalar_prefetch=1,grid=(H//2,),
       in_specs=[pl.BlockSpec((S,2*HD),lambda h,f:(0,LEAD//128+h)),pl.BlockSpec((S,2*HD),lambda h,f:(0,LEAD//128+H//2+h)),pl.BlockSpec((S,2*HD),lambda h,f:(0,LEAD//128+H+h)),
                 pl.BlockSpec((S,1),lambda h,f:(0,0)),pl.BlockSpec((1,S),lambda h,f:(0,0))],
       out_specs=[pl.BlockSpec((S,2*HD),lambda h,f:(0,h)),pl.BlockSpec((1,2,S),lambda h,f:(h,0,0))],
       scratch_shapes=[pltpu.VMEM((nq,(most+1)*T,T),jnp.float32),pltpu.VMEM((2,S,2*HD),jnp.bfloat16),pltpu.VMEM((2*HD,S),jnp.bfloat16)]),
      out_shape=[jax.ShapeDtypeStruct((S,D),jnp.bfloat16),jax.ShapeDtypeStruct((H//2,2,S),jnp.float32)],
      compiler_params=params_of(48),cost_estimate=SMALL,name="attention_forward")
    return f(first,qkv,qkv,qkv,seg.reshape(S,1),seg.reshape(1,S))

def bwd_kernel(first_ref,q_ref,k_ref,v_ref,do_ref,lse_ref,segc_ref,segr_ref,g_ref,bias,kh,kt,dk,dv,*,nq,most,scale):
    @pl.when(pl.program_id(0)==0)
    def _(): fill_bias(segc_ref,segr_ref,bias,nq,most)
    lane=lax.broadcasted_iota(jnp.int32,(1,2*HD),1)
    kh[0]=jnp.where(lane<HD,k_ref[...],0)
    kh[1]=jnp.where(lane>=HD,k_ref[...],0)
    kt[...]=k_ref[...].T
    dk[...]=jnp.zeros_like(dk); dv[...]=jnp.zeros_like(dv)
    for i in range(nq):
        hi=(i+1)*T
        qt=q_ref[i*T:hi,:]*SCALE; dot_=do_ref[i*T:hi,:]
        def variant(n):
            lo=hi-n*T
            outs=[]
            for h in range(2):
                mine=(lane<HD) if h==0 else (lane>=HD)
                qh=jnp.where(mine,qt,0); dh=jnp.where(mine,dot_,0)
                s=nt(kh[h,lo:hi,:],qt)+bias[i,(most+1-n)*T:,:]
                p=jnp.exp(s-lse_ref[0,h:h+1,i*T:hi])
                dp=nt(v_ref[lo:hi,:],dh)
                dv[lo:hi,:]+=nn(p.astype(jnp.bfloat16),dh)
                t=p*dp
                delta=jnp.sum(t,axis=0,keepdims=True)
                ds=(t-p*delta).astype(jnp.bfloat16)
                dk[lo:hi,:]+=nn(ds,qh)
                outs.append(nn(kt[h*HD:(h+1)*HD,lo:hi],ds))
            g_ref[0,i*T:hi,:]=(jnp.concatenate(outs,axis=0)*scale).T.astype(jnp.bfloat16)
        for n in range(1,min(i,most)+2):
            pl.when(first_ref[i]==n)(functools.partial(variant,n))
    g_ref[1]=dk[...].astype(jnp.bfloat16)
    g_ref[2]=dv[...].astype(jnp.bfloat16)

def attend_bwd(qkv, do, lse, seg, start, pairs, most=MOST//T):
    S=qkv.shape[0]; nq=S//T
    most=min(most,nq-1)
    first=tiles_needed(seg,nq,most)
    f=pl.pallas_call(functools.partial(bwd_kernel,nq=nq,most=most,scale=SCALE),
      grid_spec=pltpu.PrefetchScalarGridSpec(num_scalar_prefetch=1,grid=(pairs,),
       in_specs=[pl.BlockSpec((S,2*HD),lambda h,f:(0,LEAD//128+start+h)),pl.BlockSpec((S,2*HD),lambda h,f:(0,LEAD//128+H//2+start+h)),pl.BlockSpec((S,2*HD),lambda h,f:(0,LEAD//128+H+start+h)),
                 pl.BlockSpec((S,2*HD),lambda h,f:(0,start+h)),pl.BlockSpec((1,2,S),lambda h,f:(start+h,0,0)),
                 pl.BlockSpec((S,1),lambda h,f:(0,0)),pl.BlockSpec((1,S),lambda h,f:(0,0))],
       out_specs=pl.BlockSpec((3,S,2*HD),lambda h,f:(0,0,h)),
       scratch_shapes=[pltpu.VMEM((nq,(most+1)*T,T),jnp.float32),pltpu.VMEM((2,S,2*HD),jnp.bfloat16),pltpu.VMEM((2*HD,S),jnp.bfloat16),
          pltpu.VMEM((S,2*HD),jnp.float32),pltpu.VMEM((S,2*HD),jnp.float32)]),
      out_shape=jax.ShapeDtypeStruct((3,S,pairs*2*HD),jnp.bfloat16),
      compiler_params=params_of(48),cost_estimate=SMALL,name="attention_backward")
    return f(first,qkv,qkv,qkv,do,lse,seg.reshape(S,1),seg.reshape(1,S))

def after(value, *others):
    return lax.optimization_barrier((value, *others))[0]


def xor_permute(value, mask, devices):
    return lax.ppermute(value, AXES, [(i, i ^ mask) for i in range(devices)])


def by_coordinate(pieces, coordinate):
    count = len(pieces)
    index = lax.broadcasted_iota(jnp.int32, (count,) + pieces[0].shape, 0) ^ coordinate
    out = pieces[0][None]
    for m in range(1, count):
        out = jnp.where(index == m, pieces[m][None], out)
    return out


def gather_rows(mine, dp, fsdp):
    devices = dp * fsdp
    core, z = lax.axis_index("fsdp") % 2, lax.axis_index("fsdp") // 2
    part = lambda side: lax.dynamic_slice_in_dim(mine, side * HALF, HALF, axis=1)

    def spread(value, unit, count, coordinate):
        pieces = [value] + [xor_permute(value, m * unit, devices) for m in range(1, count)]
        return by_coordinate(pieces, coordinate)

    value = by_coordinate([part(core), xor_permute(part(1 - core), 1, devices)], core)
    value = spread(value, 2, fsdp // 2, z)
    value = spread(value, fsdp, dp, lax.axis_index("dp"))
    own = value.reshape(D, HALF)
    return own, xor_permute(own, 1, devices)


def add_pair(keep, got):
    return (keep.astype(jnp.float32) + got.astype(jnp.float32)).astype(jnp.bfloat16)


def add_planes(value, cover):
    value = lax.all_to_all(value, "dp", split_axis=0, concat_axis=0, tiled=True)
    return jnp.sum(after(value, cover).astype(jnp.float32), axis=0).astype(jnp.bfloat16)


def scatter_planes(value):
    return lax.psum_scatter(value, "dp", scatter_dimension=0, tiled=True)


def scatter_column(value, fsdp):
    groups = [[2 * z + c for z in range(fsdp // 2)] for c in range(2)]
    return lax.psum_scatter(
        value, "fsdp", scatter_dimension=0, axis_index_groups=groups, tiled=True
    )


def add_column(value, devices):
    chips = value.shape[0]
    z = lax.axis_index("fsdp") // 2
    take = lambda index: lax.dynamic_index_in_dim(value, index, 0, keepdims=False)
    total = take(z).astype(jnp.float32)
    for m in range(1, chips):
        total = total + xor_permute(take(z ^ m), 2 * m, devices).astype(jnp.float32)
    return total


def pack_kernel(owners_ref, grads_ref, out_ref):
    out_ref[...] = jnp.zeros_like(out_ref)
    for block in range(grads_ref.shape[1] // D):
        out_ref[owners_ref[block]] = grads_ref[:, block * D : (block + 1) * D]


def pack_blocks(owners, grads, devices):
    rows = grads.shape[0]
    return pl.pallas_call(
        pack_kernel,
        in_specs=[pl.BlockSpec(memory_space=pltpu.SMEM), pl.BlockSpec(memory_space=pltpu.VMEM)],
        out_specs=pl.BlockSpec(memory_space=pltpu.VMEM),
        out_shape=jax.ShapeDtypeStruct((devices, rows, D), jnp.bfloat16),
        name="pack_blocks",
    )(owners, grads)


def step_kernel(rate_ref, grad_ref, left_ref, right_ref, out_ref):
    half = nn(left_ref[...].astype(jnp.bfloat16), grad_ref[...]).astype(jnp.bfloat16)
    precond = nn(half, right_ref[...].astype(jnp.bfloat16))
    mean = jnp.sum(jnp.sum(precond * precond, axis=0, keepdims=True), axis=1, keepdims=True) * (
        1.0 / (D * D)
    )
    out_ref[...] = (precond * (rate_ref[0] * lax.rsqrt(mean + 1e-06))).astype(jnp.bfloat16)


def owner_step(rate, grad, left, right):
    vmem = pl.BlockSpec(memory_space=pltpu.VMEM)
    return pl.pallas_call(
        step_kernel,
        in_specs=[pl.BlockSpec(memory_space=pltpu.SMEM), vmem, vmem, vmem],
        out_specs=vmem,
        out_shape=jax.ShapeDtypeStruct((D, D), jnp.bfloat16),
        compiler_params=pltpu.CompilerParams(vmem_limit_bytes=32 * MIB),
        name="owner_step",
    )(rate.reshape(1), grad, left, right)


def update_kernel(owners_ref, step_ref, weight_ref, average_ref, new_ref, mean_ref):
    for block in range(weight_ref.shape[1] // D):
        columns = slice(block * D, (block + 1) * D)
        fresh = weight_ref[:, columns] - step_ref[owners_ref[block]].astype(jnp.float32)
        new_ref[:, columns] = fresh
        mean_ref[:, columns] = 0.9 * average_ref[:, columns] + 0.1 * fresh


def update_weights(owners, steps, weights, average):
    vmem = pl.BlockSpec(memory_space=pltpu.VMEM)
    return pl.pallas_call(
        update_kernel,
        in_specs=[pl.BlockSpec(memory_space=pltpu.SMEM), vmem, vmem, vmem],
        out_specs=[vmem, vmem],
        out_shape=[jax.ShapeDtypeStruct(weights.shape, jnp.float32)] * 2,
        compiler_params=pltpu.CompilerParams(vmem_limit_bytes=32 * MIB),
        name="update_weights",
    )(owners, steps, weights, average)


def block_rates(count):
    index = jnp.arange(count, dtype=jnp.int32)
    fc_end = 4 + FF // D
    small = 0.8 / math.sqrt(D)
    return jnp.where(
        index < 3, small, jnp.where(index == 3, 0.4, jnp.where(index < fc_end, small, 0.2))
    )


def on_device(
    dp,
    fsdp,
    tokens,
    cotangent,
    segments,
    owners,
    matrices,
    average,
    vectors,
    vec_moment,
    left_stats,
    right_stats,
    left_roots,
    right_roots,
):
    devices = dp * fsdp
    rank = lax.axis_index(AXES)
    core = (lax.axis_index("fsdp") % 2).reshape(1)
    rows_dev = matrices.shape[0]
    seg = segments[0]
    x = tokens.reshape(-1, D)
    narrow = matrices.astype(jnp.bfloat16)
    lead = jnp.pad(vectors.astype(jnp.bfloat16).T, ((0, 0), (0, LEAD - 4)))
    own, other = gather_rows(jnp.concatenate([lead, narrow[:, : 3 * D]], axis=1), dp, fsdp)
    rest = lax.all_gather(narrow[:, 3 * D :], AXES, axis=0, tiled=True)
    qkv, normed_t, params = qkv_forward(core, x, own, other)
    mixed, sums = attend_fwd(qkv, seg)
    dy = cotangent.reshape(-1, D)
    pair = lambda value: xor_permute(value, 1, devices)
    outputs, residual, slope, proj_keep, proj_send = block_forward(
        core, mixed, x, dy, rest, params, rows_dev
    )
    proj = scatter_planes(add_pair(proj_keep, pair(proj_send)))
    dx, do, sums_two, middle_keep, middle_send = block_backward(
        core, mixed, residual, dy, slope, rest, params, rows_dev
    )
    middle = scatter_planes(after(add_pair(middle_keep, pair(middle_send)), proj))
    dqkv = attend_bwd(qkv, do, sums, seg, 0, H // 2)
    late_keep, late_send = qkv_gradients(core, normed_t, dqkv, rows_dev)
    late = add_pair(late_keep, pair(late_send)).reshape(dp, fsdp // 2, rows_dev, 3 * D)
    early = scatter_column(jnp.concatenate([middle, proj], axis=1), fsdp)
    input_grad, sums_one = input_gradient(core, x, dx, after(dqkv, late), own, other, params)
    late = add_planes(late, input_grad)
    late = add_column(late, devices)
    matrix_grads = jnp.concatenate([late, early.astype(jnp.float32)], axis=1)
    bf16 = lambda value: value.astype(jnp.bfloat16)
    outgoing = pack_blocks(owners, bf16(matrix_grads), devices)
    whole = lax.all_to_all(outgoing, AXES, split_axis=0, concat_axis=0, tiled=True)
    block_grad = whole.reshape(D, D)
    mine = (owners == rank).astype(jnp.float32)
    rate = jnp.sum(mine * block_rates(owners.shape[0]))
    step = owner_step(rate, block_grad, left_roots[0], right_roots[0])
    returned = lax.all_to_all(
        step.reshape(devices, rows_dev, D), AXES, split_axis=0, concat_axis=0, tiled=True
    )
    vector_terms = jnp.concatenate([sums_one, sums_two], axis=0)
    vector_parts = lax.all_to_all(
        vector_terms.reshape(4, devices, -1).swapaxes(0, 1), AXES, split_axis=0, concat_axis=0, tiled=True
    )
    vector_grads = jnp.sum(vector_parts, axis=0)
    left_next = 0.5 * left_stats[0] + 0.5 * nt(block_grad, block_grad)
    right_next = 0.5 * right_stats[0] + 0.5 * tn(block_grad, block_grad)
    new_matrices, average_new = update_weights(owners, returned, matrices, average)
    moment_new = 0.5 * vec_moment + 0.5 * vector_grads * vector_grads
    vectors_new = vectors - 0.2 * vector_grads / (jnp.sqrt(moment_new) + 1e-08)
    return (
        outputs.reshape(tokens.shape),
        input_grad.reshape(tokens.shape),
        matrix_grads,
        vector_grads,
        left_next[None],
        right_next[None],
        new_matrices,
        moment_new,
        vectors_new,
        average_new,
    )


def solution(mesh):
    in_specs = (
        P(("dp", "fsdp"), None, None),
        P(("dp", "fsdp"), None, None),
        P(("dp", "fsdp"), None),
        P(),
        P(("dp", "fsdp"), None),
        P(("dp", "fsdp"), None),
        P(None, ("dp", "fsdp")),
        P(None, ("dp", "fsdp")),
        P(("dp", "fsdp"), None, None),
        P(("dp", "fsdp"), None, None),
        P(("dp", "fsdp"), None, None),
        P(("dp", "fsdp"), None, None),
    )
    out_specs = (
        P(("dp", "fsdp"), None, None),
        P(("dp", "fsdp"), None, None),
        P(("dp", "fsdp"), None),
        P(None, ("dp", "fsdp")),
        P(("dp", "fsdp"), None, None),
        P(("dp", "fsdp"), None, None),
        P(("dp", "fsdp"), None),
        P(None, ("dp", "fsdp")),
        P(None, ("dp", "fsdp")),
        P(("dp", "fsdp"), None),
    )
    return jax.shard_map(
        functools.partial(on_device, mesh.shape["dp"], mesh.shape["fsdp"]), mesh=mesh, in_specs=in_specs, out_specs=out_specs, check_vma=False
    )
```

```python
import functools
import math

import jax
import jax.numpy as jnp
from jax import lax
from jax.experimental import pallas as pl
from jax.experimental.pallas import tpu as pltpu
from jax.sharding import PartitionSpec as P

D = 768
H = 12
HD = 64
FF = 3072
BRANCHES = 48
BRANCH = BRANCHES ** (-0.5)
SCALE = HD ** (-0.5)
MOST = 512
T = 256
LEAD = 256
EXT = LEAD + 3 * D
HALF = EXT // 2
CHUNK = 768
NEG = -1e30
GELU_A = math.sqrt(2.0 / math.pi)
GELU_B = 0.044715
AXES = ("dp", "fsdp")
MIB = 1 << 20
SMALL = pl.CostEstimate(flops=1024, bytes_accessed=1024, transcendentals=0)


def nt(a, b):
    return lax.dot_general(a, b, (((1,), (1,)), ((), ())), preferred_element_type=jnp.float32)


def nn(a, b):
    return lax.dot_general(a, b, (((1,), (0,)), ((), ())), preferred_element_type=jnp.float32)


def tn(a, b):
    return lax.dot_general(a, b, (((0,), (0,)), ((), ())), preferred_element_type=jnp.float32)


def row_norm(rows):
    centre = rows - jnp.mean(rows, axis=-1, keepdims=True)
    inverse = lax.rsqrt(jnp.mean(centre * centre, axis=-1, keepdims=True) + 1e-05)
    return centre * inverse, inverse


def norm_backward(gradient, xhat, inverse, gain):
    e = gradient * gain
    return inverse * (
        e - jnp.mean(e, axis=-1, keepdims=True) - xhat * jnp.mean(e * xhat, axis=-1, keepdims=True)
    )


def row_sums(gradient, xhat):
    return jnp.concatenate(
        [jnp.sum(gradient * xhat, axis=0, keepdims=True), jnp.sum(gradient, axis=0, keepdims=True)],
        axis=0,
    )


def whole_spec(shape, **kwargs):
    return pl.BlockSpec(shape, lambda *_: (0,) * len(shape), **kwargs)


ONCE = dict(pipeline_mode=pl.Buffered(1))
SCALARS = pl.BlockSpec(memory_space=pltpu.SMEM)


def params_of(vmem=None):
    return pltpu.CompilerParams(vmem_limit_bytes=60 * MIB)


def qkv_kernel(core_ref, tokens_ref, own_ref, other_ref, qkv_ref, normed_ref, params_ref):
    core = core_ref[0]

    @pl.when(pl.program_id(0) == 0)
    def _():
        lead = jnp.where(core == 0, own_ref[:, :128].astype(jnp.float32), other_ref[:, :128].astype(jnp.float32))
        params_ref[...] = lead.T[:8]

    xhat, _ = row_norm(tokens_ref[...].astype(jnp.float32))
    normed = (xhat * params_ref[0:1] + params_ref[1:2]).astype(jnp.bfloat16)
    normed_ref[...] = normed.T
    for side, weights in ((core, own_ref), (1 - core, other_ref)):
        columns = pl.ds(pl.multiple_of(side * HALF, 128), HALF)
        qkv_ref[:, columns] = nn(normed, weights[...]).astype(jnp.bfloat16)


def qkv_forward(core, tokens, own, other):
    length = tokens.shape[0]
    return pl.pallas_call(
        qkv_kernel,
        grid=(length // T,),
        in_specs=[
            SCALARS,
            pl.BlockSpec((T, D), lambda i: (i, 0)),
            whole_spec((D, HALF), **ONCE),
            whole_spec((D, HALF), **ONCE),
        ],
        out_specs=[
            pl.BlockSpec((T, EXT), lambda i: (i, 0)),
            pl.BlockSpec((D, T), lambda i: (0, i)),
            whole_spec((8, D)),
        ],
        out_shape=[
            jax.ShapeDtypeStruct((length, EXT), jnp.bfloat16),
            jax.ShapeDtypeStruct((D, length), jnp.bfloat16),
            jax.ShapeDtypeStruct((8, D), jnp.float32),
        ],
        compiler_params=params_of(32),
        cost_estimate=SMALL,
        name="qkv_forward",
    )(core, tokens, own, other)


def split_rows(total, buffer, core, rows, keep_ref, send_ref):
    for part in range(total.shape[0] // rows):
        place = part // 2 * rows
        buffer[part % 2, place : place + rows] = total[part * rows : (part + 1) * rows]
    keep_ref[...] = buffer[core].astype(jnp.bfloat16)
    send_ref[...] = buffer[1 - core].astype(jnp.bfloat16)


def forward_kernel(
    rows_dev, core_ref, mixed_ref, tokens_ref, cotangent_ref, out_ref, up_ref, down_ref, params_ref,
    output_ref, residual_ref, slope_ref, keep_ref, send_ref,
    total, normed, incoming, active, buffer,
):
    step = pl.program_id(0)
    tiles = [slice(start, start + T) for start in range(0, total.shape[0], T)]

    @pl.when(step == 0)
    def _():
        for rows in tiles:
            residual = (
                tokens_ref[rows].astype(jnp.float32) + nn(mixed_ref[rows], out_ref[...]) * BRANCH
            )
            residual_ref[rows] = residual
            total[rows] = residual
            xhat, _ = row_norm(residual)
            normed[rows] = (xhat * params_ref[2:3] + params_ref[3:4]).astype(jnp.bfloat16)
            incoming[:, rows] = (cotangent_ref[rows].astype(jnp.float32) * BRANCH).astype(jnp.bfloat16).T

    for rows in tiles:
        u = nn(normed[rows], up_ref[...])
        square = u * u
        bend = jnp.tanh(u * (GELU_A + (GELU_A * GELU_B) * square))
        half = 0.5 + 0.5 * bend
        product = u * half
        hidden = product.astype(jnp.bfloat16)
        active[rows] = hidden
        slope = half + product * ((1.0 - bend) * (GELU_A + (3.0 * GELU_A * GELU_B) * square))
        slope_ref[rows] = slope.astype(jnp.bfloat16)
        total[rows] += nt(hidden, down_ref[...]) * BRANCH
    split_rows(nn(incoming[...], active[...]), buffer, core_ref[0], rows_dev, keep_ref, send_ref)

    @pl.when(step == pl.num_programs(0) - 1)
    def _():
        output_ref[...] = total[...].astype(jnp.bfloat16)


def block_forward(core, mixed, tokens, cotangent, weights, params, rows_dev):
    length = tokens.shape[0]
    parts = FF // D
    whole = whole_spec((length, D), **ONCE)
    weight = lambda first: pl.BlockSpec((D, D), lambda i: (0, first + i))
    half = pl.BlockSpec((D // 2, D), lambda i: (0, i))
    return pl.pallas_call(
        functools.partial(forward_kernel, rows_dev),
        grid=(parts,),
        in_specs=[
            SCALARS, whole, whole, whole, whole_spec((D, D), **ONCE), weight(1), weight(1 + parts),
            whole_spec((8, D)),
        ],
        out_specs=[
            whole_spec((length, D)), whole_spec((length, D)),
            pl.BlockSpec((length, D), lambda i: (0, i)), half, half,
        ],
        out_shape=[
            jax.ShapeDtypeStruct((length, D), jnp.bfloat16),
            jax.ShapeDtypeStruct((length, D), jnp.float32),
            jax.ShapeDtypeStruct((length, FF), jnp.bfloat16),
            jax.ShapeDtypeStruct((D // 2, FF), jnp.bfloat16),
            jax.ShapeDtypeStruct((D // 2, FF), jnp.bfloat16),
        ],
        scratch_shapes=[
            pltpu.VMEM((length, D), jnp.float32),
            pltpu.VMEM((length, D), jnp.bfloat16),
            pltpu.VMEM((D, length), jnp.bfloat16),
            pltpu.VMEM((length, D), jnp.bfloat16),
            pltpu.VMEM((2, D // 2, D), jnp.float32),
        ],
        compiler_params=params_of(),
        cost_estimate=SMALL,
        name="block_forward",
    )(core, mixed, tokens, cotangent, weights, weights, weights, params)


def backward_kernel(
    rows_dev, core_ref, mixed_ref, residual_ref, cotangent_ref, slope_ref, weights_ref, params_ref,
    dx_ref, do_ref, sums_ref, keep_ref, send_ref, inner, normed_t, mixed_t, outer, buffer,
):
    step = pl.program_id(0)
    tiles = inner.shape[0]
    parts = FF // CHUNK

    @pl.when(step < tiles)
    def _():
        weights = lambda block: weights_ref[:, block * D : (block + 1) * D]
        xhat, inverse = row_norm(residual_ref[...])
        normed_t[step] = (xhat * params_ref[2:3] + params_ref[3:4]).astype(jnp.bfloat16).T
        mixed_t[step] = mixed_ref[...].T
        dy = cotangent_ref[...].astype(jnp.float32)
        scaled = (dy * BRANCH).astype(jnp.bfloat16)
        dh = jnp.zeros((T, D), jnp.float32)
        for chunk in range(parts):
            columns = slice(chunk * CHUNK, (chunk + 1) * CHUNK)
            slope = slope_ref[:, columns].astype(jnp.float32)
            du = (nn(scaled, weights(1 + parts + chunk)) * slope).astype(jnp.bfloat16)
            inner[step, :, columns] = du
            dh += nt(du, weights(1 + chunk))
        both = row_sums(dh, xhat)
        sums_ref[...] = jnp.where(step == 0, both, sums_ref[...] + both)
        dx = dy + norm_backward(dh, xhat, inverse, params_ref[2:3])
        dx_ref[...] = dx
        dz = (dx * BRANCH).astype(jnp.bfloat16)
        outer[step] = dz
        do_ref[...] = nt(dz, weights(0)).astype(jnp.bfloat16)

    def gradient(left, right, columns):
        total = nn(left[0], right[0, :, columns])
        for tile in range(1, tiles):
            total += nn(left[tile], right[tile, :, columns])
        split_rows(total, buffer, core_ref[0], rows_dev, keep_ref, send_ref)

    pl.when(step == tiles)(functools.partial(gradient, mixed_t, outer, slice(0, D)))
    for chunk in range(parts):
        columns = slice(chunk * CHUNK, (chunk + 1) * CHUNK)
        pl.when(step == tiles + 1 + chunk)(functools.partial(gradient, normed_t, inner, columns))


def block_backward(core, mixed, residual, cotangent, slope, weights, params, rows_dev):
    length = residual.shape[0]
    tiles = length // T
    rows = lambda width: pl.BlockSpec((T, width), lambda i: (jnp.minimum(i, tiles - 1), 0))
    half = pl.BlockSpec((D // 2, CHUNK), lambda i: (0, jnp.maximum(i - tiles, 0)))
    return pl.pallas_call(
        functools.partial(backward_kernel, rows_dev),
        grid=(tiles + 1 + FF // CHUNK,),
        in_specs=[
            SCALARS, rows(D), rows(D), rows(D), rows(FF), whole_spec(weights.shape, **ONCE),
            whole_spec((8, D)),
        ],
        out_specs=[rows(D), rows(D), whole_spec((2, D)), half, half],
        out_shape=[
            jax.ShapeDtypeStruct((length, D), jnp.float32),
            jax.ShapeDtypeStruct((length, D), jnp.bfloat16),
            jax.ShapeDtypeStruct((2, D), jnp.float32),
            jax.ShapeDtypeStruct((D // 2, D + FF), jnp.bfloat16),
            jax.ShapeDtypeStruct((D // 2, D + FF), jnp.bfloat16),
        ],
        scratch_shapes=[
            pltpu.VMEM((tiles, T, FF), jnp.bfloat16),
            pltpu.VMEM((tiles, D, T), jnp.bfloat16),
            pltpu.VMEM((tiles, D, T), jnp.bfloat16),
            pltpu.VMEM((tiles, T, D), jnp.bfloat16),
            pltpu.VMEM((2, D // 2, CHUNK), jnp.float32),
        ],
        compiler_params=params_of(52),
        cost_estimate=SMALL,
        name="block_backward",
    )(core, mixed, residual, cotangent, slope, weights, params)


def qkv_grad_kernel(rows_dev, core_ref, normed_ref, dqkv_ref, keep_ref, send_ref, buffer):
    split_rows(nn(normed_ref[...], dqkv_ref[0]), buffer, core_ref[0], rows_dev, keep_ref, send_ref)


def qkv_gradients(core, normed_t, dqkv, rows_dev):
    length = normed_t.shape[1]
    half = pl.BlockSpec((D // 2, D), lambda t: (0, t))
    return pl.pallas_call(
        functools.partial(qkv_grad_kernel, rows_dev),
        grid=(3,),
        in_specs=[
            SCALARS, whole_spec((D, length), **ONCE), pl.BlockSpec((1, length, D), lambda t: (t, 0, 0)),
        ],
        out_specs=[half, half],
        out_shape=[jax.ShapeDtypeStruct((D // 2, 3 * D), jnp.bfloat16)] * 2,
        scratch_shapes=[pltpu.VMEM((2, D // 2, D), jnp.float32)],
        compiler_params=params_of(40),
        cost_estimate=SMALL,
        name="qkv_gradients",
    )(core, normed_t, dqkv)


def input_kernel(
    core_ref, tokens_ref, dx_ref, dqkv_ref, own_ref, other_ref, params_ref,
    out_ref, sums_ref, wide,
):
    core = core_ref[0]
    wide[:, :LEAD] = jnp.zeros((T, LEAD), jnp.bfloat16)
    for t in range(3):
        wide[:, LEAD + t * D : LEAD + (t + 1) * D] = dqkv_ref[t]
    place = lambda side: pl.ds(pl.multiple_of(side * HALF, 128), HALF)
    dh = nt(wide[:, place(core)], own_ref[...]) + nt(wide[:, place(1 - core)], other_ref[...])
    xhat, inverse = row_norm(tokens_ref[...].astype(jnp.float32))
    both = row_sums(dh, xhat)
    sums_ref[...] = jnp.where(pl.program_id(0) == 0, both, sums_ref[...] + both)
    out_ref[...] = (dx_ref[...] + norm_backward(dh, xhat, inverse, params_ref[0:1])).astype(jnp.bfloat16)


def input_gradient(core, tokens, dx, dqkv, own, other, params):
    length = tokens.shape[0]
    rows = pl.BlockSpec((T, D), lambda i: (i, 0))
    return pl.pallas_call(
        input_kernel,
        grid=(length // T,),
        in_specs=[
            SCALARS, rows, rows, pl.BlockSpec((3, T, D), lambda i: (0, i, 0)),
            whole_spec((D, HALF), **ONCE), whole_spec((D, HALF), **ONCE), whole_spec((8, D)),
        ],
        out_specs=[rows, whole_spec((2, D))],
        out_shape=[
            jax.ShapeDtypeStruct((length, D), jnp.bfloat16),
            jax.ShapeDtypeStruct((2, D), jnp.float32),
        ],
        scratch_shapes=[pltpu.VMEM((T, EXT), jnp.bfloat16)],
        compiler_params=params_of(32),
        cost_estimate=SMALL,
        name="input_gradient",
    )(core, tokens, dx, dqkv, own, other, params)


def fill_bias(segc_ref, segr_ref, bias, nq, most):
    for i in range(nq):
        for d in range(most+1):
            j=i-most+d
            if j<0: continue
            same = segc_ref[j*T:(j+1)*T,:] == segr_ref[:, i*T:(i+1)*T]
            if j==i:
                kp=lax.broadcasted_iota(jnp.int32,(T,T),0); qp=lax.broadcasted_iota(jnp.int32,(T,T),1)
                same = same & (kp<=qp)
            bias[i, d*T:(d+1)*T, :] = jnp.where(same,0.0,NEG)

def fwd_kernel(first_ref, q_ref,k_ref,v_ref,segc_ref,segr_ref,o_ref,lse_ref,bias,kh,vt,*,nq,most):
    @pl.when(pl.program_id(0)==0)
    def _(): fill_bias(segc_ref,segr_ref,bias,nq,most)
    lane=lax.broadcasted_iota(jnp.int32,(1,2*HD),1)
    kh[0]=jnp.where(lane<HD,k_ref[...],0)
    kh[1]=jnp.where(lane>=HD,k_ref[...],0)
    vt[...]=v_ref[...].T
    for i in range(nq):
        hi=(i+1)*T
        qt=q_ref[i*T:hi,:]*SCALE
        def variant(n):
            lo=hi-n*T
            outs=[]
            for h in range(2):
                s=nt(kh[h,lo:hi,:],qt)+bias[i,(most+1-n)*T:,:]
                top=jnp.max(s,axis=0,keepdims=True)
                e=jnp.exp(s-top)
                tot=jnp.sum(e,axis=0,keepdims=True)
                ot=nn(vt[h*HD:(h+1)*HD,lo:hi],e.astype(jnp.bfloat16))
                outs.append(ot*(1.0/tot))
                lse_ref[0,h:h+1,i*T:hi]=top+jnp.log(tot)
            o_ref[i*T:hi,:]=jnp.concatenate(outs,axis=0).T.astype(jnp.bfloat16)
        for n in range(1,min(i,most)+2):
            pl.when(first_ref[i]==n)(functools.partial(variant,n))

def tiles_needed(seg, nq, most):
    last=seg[T-1::T]; first=seg[0::T]
    j=jnp.arange(nq)
    need=(last[None,:]>=first[:,None])&(j[None,:]<=j[:,None])
    return jnp.sum(need,axis=1).astype(jnp.int32)

def attend_fwd(qkv, seg, most=MOST//T):
    S=qkv.shape[0]; nq=S//T
    most=min(most,nq-1)
    first=tiles_needed(seg,nq,most)
    f=pl.pallas_call(functools.partial(fwd_kernel,nq=nq,most=most),
      grid_spec=pltpu.PrefetchScalarGridSpec(num_scalar_prefetch=1,grid=(H//2,),
       in_specs=[pl.BlockSpec((S,2*HD),lambda h,f:(0,LEAD//128+h)),pl.BlockSpec((S,2*HD),lambda h,f:(0,LEAD//128+H//2+h)),pl.BlockSpec((S,2*HD),lambda h,f:(0,LEAD//128+H+h)),
                 pl.BlockSpec((S,1),lambda h,f:(0,0)),pl.BlockSpec((1,S),lambda h,f:(0,0))],
       out_specs=[pl.BlockSpec((S,2*HD),lambda h,f:(0,h)),pl.BlockSpec((1,2,S),lambda h,f:(h,0,0))],
       scratch_shapes=[pltpu.VMEM((nq,(most+1)*T,T),jnp.float32),pltpu.VMEM((2,S,2*HD),jnp.bfloat16),pltpu.VMEM((2*HD,S),jnp.bfloat16)]),
      out_shape=[jax.ShapeDtypeStruct((S,D),jnp.bfloat16),jax.ShapeDtypeStruct((H//2,2,S),jnp.float32)],
      compiler_params=params_of(48),cost_estimate=SMALL,name="attention_forward")
    return f(first,qkv,qkv,qkv,seg.reshape(S,1),seg.reshape(1,S))

PAIRS = 2
PAIR = 2 * HD


def bwd_kernel(
    first_ref, q_ref, k_ref, v_ref, do_ref, o_ref, lse_ref, segc_ref, segr_ref, g_ref,
    bias, key, key_t, key_grad, value_grad, *, nq, most,
):
    @pl.when(pl.program_id(0) == 0)
    def _():
        fill_bias(segc_ref, segr_ref, bias, nq, most)

    lane = lax.broadcasted_iota(jnp.int32, (1, PAIR), 1)
    mine = (lane < HD, lane >= HD)
    groups = [slice(pair * PAIR, (pair + 1) * PAIR) for pair in range(PAIRS)]
    for pair, lanes in enumerate(groups):
        for h in range(2):
            key[2 * pair + h] = jnp.where(mine[h], k_ref[:, lanes], 0)
    key_t[...] = k_ref[...].T
    key_grad[...] = jnp.zeros_like(key_grad)
    value_grad[...] = jnp.zeros_like(value_grad)
    for i in range(nq):
        rows = slice(i * T, (i + 1) * T)

        def variant(n, i=i, rows=rows):
            keys = slice((i + 1 - n) * T, (i + 1) * T)
            mask = bias[i, (most + 1 - n) * T :, :]
            for pair, lanes in enumerate(groups):
                query = q_ref[rows, lanes] * SCALE
                grad = do_ref[rows, lanes]
                meet = (grad.astype(jnp.float32) * o_ref[rows, lanes].astype(jnp.float32)).T
                outs = []
                for h in range(2):
                    head = 2 * pair + h
                    query_h = jnp.where(mine[h], query, 0)
                    grad_h = jnp.where(mine[h], grad, 0)
                    scores = nt(key[head, keys, :], query) + mask
                    probs = jnp.exp(scores - lse_ref[pair, h : h + 1, rows])
                    prob_grad = nt(v_ref[keys, lanes], grad_h)
                    value_grad[keys, lanes] += nn(probs.astype(jnp.bfloat16), grad_h)
                    delta = jnp.sum(meet[h * HD : (h + 1) * HD], axis=0, keepdims=True)
                    score_grad = (probs * (prob_grad - delta)).astype(jnp.bfloat16)
                    key_grad[keys, lanes] += nn(score_grad, query_h)
                    outs.append(nn(key_t[head * HD : (head + 1) * HD, keys], score_grad))
                total = jnp.concatenate(outs, axis=0) * SCALE
                g_ref[0, rows, lanes] = total.T.astype(jnp.bfloat16)

        for n in range(1, min(i, most) + 2):
            pl.when(first_ref[i] == n)(functools.partial(variant, n))
    g_ref[1] = key_grad[...].astype(jnp.bfloat16)
    g_ref[2] = value_grad[...].astype(jnp.bfloat16)


def attend_bwd(qkv, grad, out, lse, seg):
    length = qkv.shape[0]
    nq = length // T
    most = min(MOST // T, nq - 1)
    wide = PAIRS * PAIR
    steps = D // wide
    first = tiles_needed(seg, nq, most)
    columns = lambda start: pl.BlockSpec((length, wide), lambda h, f: (0, start // wide + h))
    return pl.pallas_call(
        functools.partial(bwd_kernel, nq=nq, most=most),
        grid_spec=pltpu.PrefetchScalarGridSpec(
            num_scalar_prefetch=1,
            grid=(steps,),
            in_specs=[
                columns(LEAD), columns(LEAD + D), columns(LEAD + 2 * D), columns(0), columns(0),
                pl.BlockSpec((PAIRS, 2, length), lambda h, f: (h, 0, 0)),
                whole_spec((length, 1)), whole_spec((1, length)),
            ],
            out_specs=pl.BlockSpec((3, length, wide), lambda h, f: (0, 0, h)),
            scratch_shapes=[
                pltpu.VMEM((nq, (most + 1) * T, T), jnp.float32),
                pltpu.VMEM((2 * PAIRS, length, PAIR), jnp.bfloat16),
                pltpu.VMEM((wide, length), jnp.bfloat16),
                pltpu.VMEM((length, wide), jnp.float32),
                pltpu.VMEM((length, wide), jnp.float32),
            ],
        ),
        out_shape=jax.ShapeDtypeStruct((3, length, D), jnp.bfloat16),
        compiler_params=params_of(),
        cost_estimate=SMALL,
        name="attention_backward",
    )(first, qkv, qkv, qkv, grad, out, lse, seg.reshape(length, 1), seg.reshape(1, length))


def after(value, *others):
    return lax.optimization_barrier((value, *others))[0]


def xor_permute(value, mask, devices):
    return lax.ppermute(value, AXES, [(i, i ^ mask) for i in range(devices)])


def by_coordinate(pieces, coordinate):
    count = len(pieces)
    index = lax.broadcasted_iota(jnp.int32, (count,) + pieces[0].shape, 0) ^ coordinate
    out = pieces[0][None]
    for m in range(1, count):
        out = jnp.where(index == m, pieces[m][None], out)
    return out


def gather_rows(mine, dp, fsdp):
    devices = dp * fsdp
    core, z = lax.axis_index("fsdp") % 2, lax.axis_index("fsdp") // 2
    part = lambda side: lax.dynamic_slice_in_dim(mine, side * HALF, HALF, axis=1)

    def spread(value, unit, count, coordinate):
        pieces = [value] + [xor_permute(value, m * unit, devices) for m in range(1, count)]
        return by_coordinate(pieces, coordinate)

    value = by_coordinate([part(core), xor_permute(part(1 - core), 1, devices)], core)
    value = spread(value, 2, fsdp // 2, z)
    value = spread(value, fsdp, dp, lax.axis_index("dp"))
    own = value.reshape(D, HALF)
    return own, xor_permute(own, 1, devices)


def add_pair(keep, got):
    return (keep.astype(jnp.float32) + got.astype(jnp.float32)).astype(jnp.bfloat16)


def add_planes(value, cover):
    value = lax.all_to_all(value, "dp", split_axis=0, concat_axis=0, tiled=True)
    return jnp.sum(after(value, cover).astype(jnp.float32), axis=0).astype(jnp.bfloat16)


def scatter_planes(value):
    return lax.psum_scatter(value, "dp", scatter_dimension=0, tiled=True)


def scatter_column(value, fsdp):
    groups = [[2 * z + c for z in range(fsdp // 2)] for c in range(2)]
    return lax.psum_scatter(
        value, "fsdp", scatter_dimension=0, axis_index_groups=groups, tiled=True
    )


def add_column(value, devices):
    chips = value.shape[0]
    z = lax.axis_index("fsdp") // 2
    take = lambda index: lax.dynamic_index_in_dim(value, index, 0, keepdims=False)
    total = take(z).astype(jnp.float32)
    for m in range(1, chips):
        total = total + xor_permute(take(z ^ m), 2 * m, devices).astype(jnp.float32)
    return total


def pack_kernel(owners_ref, late_ref, early_ref, grads_ref, out_ref):
    out_ref[...] = jnp.zeros_like(out_ref)
    late = late_ref.shape[1]
    grads_ref[:, :late] = late_ref[...]
    grads_ref[:, late:] = early_ref[...].astype(jnp.float32)
    for block in range(grads_ref.shape[1] // D):
        columns = slice(block * D, (block + 1) * D)
        out_ref[owners_ref[block]] = grads_ref[:, columns].astype(jnp.bfloat16)


def pack_blocks(owners, late, early, devices):
    rows = late.shape[0]
    vmem = pl.BlockSpec(memory_space=pltpu.VMEM)
    return pl.pallas_call(
        pack_kernel,
        in_specs=[SCALARS, vmem, vmem],
        out_specs=[vmem, vmem],
        out_shape=[
            jax.ShapeDtypeStruct((rows, late.shape[1] + early.shape[1]), jnp.float32),
            jax.ShapeDtypeStruct((devices, rows, D), jnp.bfloat16),
        ],
        compiler_params=pltpu.CompilerParams(vmem_limit_bytes=16 * MIB),
        cost_estimate=SMALL,
        name="pack_blocks",
    )(owners, late, early)


def step_kernel(rate_ref, grad_ref, left_ref, right_ref, out_ref):
    half = nn(left_ref[...], grad_ref[...]).astype(jnp.bfloat16)
    precond = nn(half, right_ref[...])
    mean = jnp.sum(jnp.sum(precond * precond, axis=0, keepdims=True), axis=1, keepdims=True) * (
        1.0 / (D * D)
    )
    out_ref[...] = (precond * (rate_ref[0] * lax.rsqrt(mean + 1e-06))).astype(jnp.bfloat16)


def owner_step(rate, grad, left, right):
    vmem = pl.BlockSpec(memory_space=pltpu.VMEM)
    return pl.pallas_call(
        step_kernel,
        in_specs=[pl.BlockSpec(memory_space=pltpu.SMEM), vmem, vmem, vmem],
        out_specs=vmem,
        out_shape=jax.ShapeDtypeStruct((D, D), jnp.bfloat16),
        compiler_params=pltpu.CompilerParams(vmem_limit_bytes=24 * MIB),
        name="owner_step",
    )(rate.reshape(1), grad, left, right)


def update_kernel(owners_ref, step_ref, weight_ref, average_ref, new_ref, mean_ref):
    for block in range(weight_ref.shape[1] // D):
        columns = slice(block * D, (block + 1) * D)
        fresh = weight_ref[:, columns] - step_ref[owners_ref[block]].astype(jnp.float32)
        new_ref[:, columns] = fresh
        mean_ref[:, columns] = 0.9 * average_ref[:, columns] + 0.1 * fresh


def update_weights(owners, steps, weights, average):
    vmem = pl.BlockSpec(memory_space=pltpu.VMEM)
    return pl.pallas_call(
        update_kernel,
        in_specs=[pl.BlockSpec(memory_space=pltpu.SMEM), vmem, vmem, vmem],
        out_specs=[vmem, vmem],
        out_shape=[jax.ShapeDtypeStruct(weights.shape, jnp.float32)] * 2,
        compiler_params=pltpu.CompilerParams(vmem_limit_bytes=16 * MIB),
        name="update_weights",
    )(owners, steps, weights, average)


def block_rates(count):
    index = jnp.arange(count, dtype=jnp.int32)
    fc_end = 4 + FF // D
    small = 0.8 / math.sqrt(D)
    return jnp.where(
        index < 3, small, jnp.where(index == 3, 0.4, jnp.where(index < fc_end, small, 0.2))
    )


def on_device(
    dp,
    fsdp,
    tokens,
    cotangent,
    segments,
    owners,
    matrices,
    average,
    vectors,
    vec_moment,
    left_stats,
    right_stats,
    left_roots,
    right_roots,
):
    devices = dp * fsdp
    rank = lax.axis_index(AXES)
    core = (lax.axis_index("fsdp") % 2).reshape(1)
    rows_dev = matrices.shape[0]
    seg = segments[0]
    x = tokens.reshape(-1, D)
    narrow = matrices.astype(jnp.bfloat16)
    lead = jnp.pad(vectors.astype(jnp.bfloat16).T, ((0, 0), (0, LEAD - 4)))
    own, other = gather_rows(jnp.concatenate([lead, narrow[:, : 3 * D]], axis=1), dp, fsdp)
    rest = lax.all_gather(narrow[:, 3 * D :], AXES, axis=0, tiled=True)
    qkv, normed_t, params = qkv_forward(core, x, own, other)
    mixed, sums = attend_fwd(qkv, seg)
    dy = cotangent.reshape(-1, D)
    pair = lambda value: xor_permute(value, 1, devices)
    outputs, residual, slope, proj_keep, proj_send = block_forward(
        core, mixed, x, dy, rest, params, rows_dev
    )
    proj = scatter_planes(add_pair(proj_keep, pair(proj_send)))
    dx, do, sums_two, middle_keep, middle_send = block_backward(
        core, mixed, residual, dy, slope, rest, params, rows_dev
    )
    middle = scatter_planes(after(add_pair(middle_keep, pair(middle_send)), proj))
    dqkv = attend_bwd(qkv, do, mixed, sums, seg)
    late_keep, late_send = qkv_gradients(core, normed_t, dqkv, rows_dev)
    late = add_pair(late_keep, pair(late_send)).reshape(dp, fsdp // 2, rows_dev, 3 * D)
    early = jnp.concatenate([after(middle, late), proj], axis=1)
    input_grad, sums_one = input_gradient(core, x, dx, after(dqkv, early), own, other, params)
    early = scatter_column(early, fsdp)
    late = add_planes(late, input_grad)
    late = add_column(late, devices)
    vector_terms = jnp.concatenate([sums_one, sums_two], axis=0)
    vector_terms = vector_terms.reshape(4, devices, -1).swapaxes(0, 1)
    vector_parts = lax.all_to_all(vector_terms, AXES, split_axis=0, concat_axis=0, tiled=True)
    vector_grads = jnp.sum(vector_parts, axis=0)
    late = after(late, vector_grads)
    matrix_grads, outgoing = pack_blocks(owners, late, early, devices)
    bf16 = lambda value: value.astype(jnp.bfloat16)
    left_root, right_root = bf16(after(left_roots[0], outgoing)), bf16(after(right_roots[0], outgoing))
    whole = lax.all_to_all(outgoing, AXES, split_axis=0, concat_axis=0, tiled=True)
    block_grad = whole.reshape(D, D)
    mine = (owners == rank).astype(jnp.float32)
    rate = jnp.sum(mine * block_rates(owners.shape[0]))
    step = owner_step(rate, block_grad, left_root, right_root)
    returned = lax.all_to_all(
        step.reshape(devices, rows_dev, D), AXES, split_axis=0, concat_axis=0, tiled=True
    )
    left_next = 0.5 * left_stats[0] + 0.5 * nt(block_grad, block_grad)
    right_next = 0.5 * right_stats[0] + 0.5 * tn(block_grad, block_grad)
    new_matrices, average_new = update_weights(owners, returned, matrices, average)
    moment_new = 0.5 * vec_moment + 0.5 * vector_grads * vector_grads
    vectors_new = vectors - 0.2 * vector_grads / (jnp.sqrt(moment_new) + 1e-08)
    return (
        outputs.reshape(tokens.shape),
        input_grad.reshape(tokens.shape),
        matrix_grads,
        vector_grads,
        left_next[None],
        right_next[None],
        new_matrices,
        moment_new,
        vectors_new,
        average_new,
    )


def solution(mesh):
    in_specs = (
        P(("dp", "fsdp"), None, None),
        P(("dp", "fsdp"), None, None),
        P(("dp", "fsdp"), None),
        P(),
        P(("dp", "fsdp"), None),
        P(("dp", "fsdp"), None),
        P(None, ("dp", "fsdp")),
        P(None, ("dp", "fsdp")),
        P(("dp", "fsdp"), None, None),
        P(("dp", "fsdp"), None, None),
        P(("dp", "fsdp"), None, None),
        P(("dp", "fsdp"), None, None),
    )
    out_specs = (
        P(("dp", "fsdp"), None, None),
        P(("dp", "fsdp"), None, None),
        P(("dp", "fsdp"), None),
        P(None, ("dp", "fsdp")),
        P(("dp", "fsdp"), None, None),
        P(("dp", "fsdp"), None, None),
        P(("dp", "fsdp"), None),
        P(None, ("dp", "fsdp")),
        P(None, ("dp", "fsdp")),
        P(("dp", "fsdp"), None),
    )
    return jax.shard_map(
        functools.partial(on_device, mesh.shape["dp"], mesh.shape["fsdp"]), mesh=mesh, in_specs=in_specs, out_specs=out_specs, check_vma=False
    )
```

```python
import functools
import math

import jax
import jax.numpy as jnp
from jax import lax
from jax.experimental import pallas as pl
from jax.experimental.pallas import tpu as pltpu
from jax.sharding import PartitionSpec as P

D = 768
H = 12
HD = 64
FF = 3072
BRANCHES = 48
BRANCH = BRANCHES ** (-0.5)
SCALE = HD ** (-0.5)
MOST = 512
T = 256
LEAD = 256
EXT = LEAD + 3 * D
HALF = EXT // 2
CHUNK = 768
NEG = -1e30
GELU_A = math.sqrt(2.0 / math.pi)
GELU_B = 0.044715
AXES = ("dp", "fsdp")
MIB = 1 << 20
SMALL = pl.CostEstimate(flops=1024, bytes_accessed=1024, transcendentals=0)


def nt(a, b):
    return lax.dot_general(a, b, (((1,), (1,)), ((), ())), preferred_element_type=jnp.float32)


def nn(a, b):
    return lax.dot_general(a, b, (((1,), (0,)), ((), ())), preferred_element_type=jnp.float32)


def tn(a, b):
    return lax.dot_general(a, b, (((0,), (0,)), ((), ())), preferred_element_type=jnp.float32)


def row_norm(rows):
    centre = rows - jnp.mean(rows, axis=-1, keepdims=True)
    inverse = lax.rsqrt(jnp.mean(centre * centre, axis=-1, keepdims=True) + 1e-05)
    return centre * inverse, inverse


def norm_backward(gradient, xhat, inverse, gain):
    e = gradient * gain
    return inverse * (
        e - jnp.mean(e, axis=-1, keepdims=True) - xhat * jnp.mean(e * xhat, axis=-1, keepdims=True)
    )


def row_sums(gradient, xhat):
    return jnp.concatenate(
        [jnp.sum(gradient * xhat, axis=0, keepdims=True), jnp.sum(gradient, axis=0, keepdims=True)],
        axis=0,
    )


def whole_spec(shape, **kwargs):
    return pl.BlockSpec(shape, lambda *_: (0,) * len(shape), **kwargs)


ONCE = dict(pipeline_mode=pl.Buffered(1))
SCALARS = pl.BlockSpec(memory_space=pltpu.SMEM)


def params_of(vmem=None):
    return pltpu.CompilerParams(vmem_limit_bytes=60 * MIB)


def qkv_kernel(core_ref, tokens_ref, own_ref, other_ref, qkv_ref, normed_ref, params_ref):
    core = core_ref[0]

    @pl.when(pl.program_id(0) == 0)
    def _():
        lead = jnp.where(core == 0, own_ref[:, :128].astype(jnp.float32), other_ref[:, :128].astype(jnp.float32))
        params_ref[...] = lead.T[:8]

    xhat, _ = row_norm(tokens_ref[...].astype(jnp.float32))
    normed = (xhat * params_ref[0:1] + params_ref[1:2]).astype(jnp.bfloat16)
    normed_ref[...] = normed.T
    for side, weights in ((core, own_ref), (1 - core, other_ref)):
        columns = pl.ds(pl.multiple_of(side * HALF, 128), HALF)
        qkv_ref[:, columns] = nn(normed, weights[...]).astype(jnp.bfloat16)


def qkv_forward(core, tokens, own, other):
    length = tokens.shape[0]
    return pl.pallas_call(
        qkv_kernel,
        grid=(length // T,),
        in_specs=[
            SCALARS,
            pl.BlockSpec((T, D), lambda i: (i, 0)),
            whole_spec((D, HALF), **ONCE),
            whole_spec((D, HALF), **ONCE),
        ],
        out_specs=[
            pl.BlockSpec((T, EXT), lambda i: (i, 0)),
            pl.BlockSpec((D, T), lambda i: (0, i)),
            whole_spec((8, D)),
        ],
        out_shape=[
            jax.ShapeDtypeStruct((length, EXT), jnp.bfloat16),
            jax.ShapeDtypeStruct((D, length), jnp.bfloat16),
            jax.ShapeDtypeStruct((8, D), jnp.float32),
        ],
        compiler_params=params_of(32),
        cost_estimate=SMALL,
        name="qkv_forward",
    )(core, tokens, own, other)


def split_rows(total, buffer, core, rows, keep_ref, send_ref):
    for part in range(total.shape[0] // rows):
        place = part // 2 * rows
        buffer[part % 2, place : place + rows] = total[part * rows : (part + 1) * rows]
    keep_ref[...] = buffer[core].astype(jnp.bfloat16)
    send_ref[...] = buffer[1 - core].astype(jnp.bfloat16)


def forward_kernel(
    rows_dev, core_ref, mixed_ref, tokens_ref, cotangent_ref, out_ref, up_ref, params_ref,
    residual_ref, active_ref, slope_ref, keep_ref, send_ref, normed, incoming, buffer,
):
    step = pl.program_id(0)
    tiles = [slice(start, start + T) for start in range(0, normed.shape[0], T)]

    @pl.when(step == 0)
    def _():
        for rows in tiles:
            residual = (
                tokens_ref[rows].astype(jnp.float32) + nn(mixed_ref[rows], out_ref[...]) * BRANCH
            )
            residual_ref[rows] = residual
            xhat, _ = row_norm(residual)
            normed[rows] = (xhat * params_ref[2:3] + params_ref[3:4]).astype(jnp.bfloat16)
            incoming[:, rows] = (cotangent_ref[rows].astype(jnp.float32) * BRANCH).astype(jnp.bfloat16).T

    for rows in tiles:
        u = nn(normed[rows], up_ref[...])
        square = u * u
        bend = jnp.tanh(u * (GELU_A + (GELU_A * GELU_B) * square))
        half = 0.5 + 0.5 * bend
        product = u * half
        active_ref[rows] = product.astype(jnp.bfloat16)
        slope = half + product * ((1.0 - bend) * (GELU_A + (3.0 * GELU_A * GELU_B) * square))
        slope_ref[rows] = slope.astype(jnp.bfloat16)
    split_rows(nn(incoming[...], active_ref[...]), buffer, core_ref[0], rows_dev, keep_ref, send_ref)


def block_forward(core, mixed, tokens, cotangent, weights, params, rows_dev):
    length = tokens.shape[0]
    parts = FF // D
    whole = whole_spec((length, D), **ONCE)
    weight = lambda first: pl.BlockSpec((D, D), lambda i: (0, first + i))
    half = pl.BlockSpec((D // 2, D), lambda i: (0, i))
    return pl.pallas_call(
        functools.partial(forward_kernel, rows_dev),
        grid=(parts,),
        in_specs=[
            SCALARS, whole, whole, whole, whole_spec((D, D), **ONCE), weight(1),
            whole_spec((8, D)),
        ],
        out_specs=[
            whole_spec((length, D)), pl.BlockSpec((length, D), lambda i: (0, i)),
            pl.BlockSpec((length, D), lambda i: (0, i)), half, half,
        ],
        out_shape=[
            jax.ShapeDtypeStruct((length, D), jnp.float32),
            jax.ShapeDtypeStruct((length, FF), jnp.bfloat16),
            jax.ShapeDtypeStruct((length, FF), jnp.bfloat16),
            jax.ShapeDtypeStruct((D // 2, FF), jnp.bfloat16),
            jax.ShapeDtypeStruct((D // 2, FF), jnp.bfloat16),
        ],
        scratch_shapes=[
            pltpu.VMEM((length, D), jnp.bfloat16),
            pltpu.VMEM((D, length), jnp.bfloat16),
            pltpu.VMEM((2, D // 2, D), jnp.float32),
        ],
        compiler_params=params_of(),
        cost_estimate=SMALL,
        name="block_forward",
    )(core, mixed, tokens, cotangent, weights, weights, params)


def output_kernel(residual_ref, active_ref, *refs):
    total = residual_ref[...]
    for part, down_ref in enumerate(refs[:-1]):
        total += nt(active_ref[:, part * D : (part + 1) * D], down_ref[...]) * BRANCH
    refs[-1][...] = total.astype(jnp.bfloat16)


def block_outputs(residual, active, weights):
    length = residual.shape[0]
    parts = FF // D
    rows = lambda width: pl.BlockSpec((T, width), lambda i: (i, 0))
    down = [
        pl.BlockSpec((D, D), lambda i, part=part: (0, 1 + parts + part), **ONCE) for part in range(parts)
    ]
    return pl.pallas_call(
        output_kernel,
        grid=(length // T,),
        in_specs=[rows(D), rows(FF), *down],
        out_specs=rows(D),
        out_shape=jax.ShapeDtypeStruct((length, D), jnp.bfloat16),
        compiler_params=params_of(),
        cost_estimate=SMALL,
        name="block_outputs",
    )(residual, active, *[weights] * parts)


def backward_kernel(
    rows_dev, core_ref, mixed_ref, residual_ref, cotangent_ref, slope_ref, weights_ref, params_ref,
    dx_ref, do_ref, sums_ref, keep_ref, send_ref, inner, normed_t, mixed_t, outer, buffer,
):
    step = pl.program_id(0)
    tiles = inner.shape[0]
    parts = FF // CHUNK

    @pl.when(step < tiles)
    def _():
        weights = lambda block: weights_ref[:, block * D : (block + 1) * D]
        xhat, inverse = row_norm(residual_ref[...])
        normed_t[step] = (xhat * params_ref[2:3] + params_ref[3:4]).astype(jnp.bfloat16).T
        mixed_t[step] = mixed_ref[...].T
        dy = cotangent_ref[...].astype(jnp.float32)
        scaled = (dy * BRANCH).astype(jnp.bfloat16)
        dh = jnp.zeros((T, D), jnp.float32)
        for chunk in range(parts):
            columns = slice(chunk * CHUNK, (chunk + 1) * CHUNK)
            slope = slope_ref[:, columns].astype(jnp.float32)
            du = (nn(scaled, weights(1 + parts + chunk)) * slope).astype(jnp.bfloat16)
            inner[step, :, columns] = du
            dh += nt(du, weights(1 + chunk))
        both = row_sums(dh, xhat)
        sums_ref[...] = jnp.where(step == 0, both, sums_ref[...] + both)
        dx = dy + norm_backward(dh, xhat, inverse, params_ref[2:3])
        dx_ref[...] = dx
        dz = (dx * BRANCH).astype(jnp.bfloat16)
        outer[step] = dz
        do_ref[...] = nt(dz, weights(0)).astype(jnp.bfloat16)

    def gradient(left, right, columns):
        total = nn(left[0], right[0, :, columns])
        for tile in range(1, tiles):
            total += nn(left[tile], right[tile, :, columns])
        split_rows(total, buffer, core_ref[0], rows_dev, keep_ref, send_ref)

    pl.when(step == tiles)(functools.partial(gradient, mixed_t, outer, slice(0, D)))
    for chunk in range(parts):
        columns = slice(chunk * CHUNK, (chunk + 1) * CHUNK)
        pl.when(step == tiles + 1 + chunk)(functools.partial(gradient, normed_t, inner, columns))


def block_backward(core, mixed, residual, cotangent, slope, weights, params, rows_dev):
    length = residual.shape[0]
    tiles = length // T
    rows = lambda width: pl.BlockSpec((T, width), lambda i: (jnp.minimum(i, tiles - 1), 0))
    half = pl.BlockSpec((D // 2, CHUNK), lambda i: (0, jnp.maximum(i - tiles, 0)))
    return pl.pallas_call(
        functools.partial(backward_kernel, rows_dev),
        grid=(tiles + 1 + FF // CHUNK,),
        in_specs=[
            SCALARS, rows(D), rows(D), rows(D), rows(FF), whole_spec(weights.shape, **ONCE),
            whole_spec((8, D)),
        ],
        out_specs=[rows(D), rows(D), whole_spec((2, D)), half, half],
        out_shape=[
            jax.ShapeDtypeStruct((length, D), jnp.float32),
            jax.ShapeDtypeStruct((length, D), jnp.bfloat16),
            jax.ShapeDtypeStruct((2, D), jnp.float32),
            jax.ShapeDtypeStruct((D // 2, D + FF), jnp.bfloat16),
            jax.ShapeDtypeStruct((D // 2, D + FF), jnp.bfloat16),
        ],
        scratch_shapes=[
            pltpu.VMEM((tiles, T, FF), jnp.bfloat16),
            pltpu.VMEM((tiles, D, T), jnp.bfloat16),
            pltpu.VMEM((tiles, D, T), jnp.bfloat16),
            pltpu.VMEM((tiles, T, D), jnp.bfloat16),
            pltpu.VMEM((2, D // 2, CHUNK), jnp.float32),
        ],
        compiler_params=params_of(52),
        cost_estimate=SMALL,
        name="block_backward",
    )(core, mixed, residual, cotangent, slope, weights, params)


def qkv_grad_kernel(rows_dev, core_ref, normed_ref, dqkv_ref, keep_ref, send_ref, buffer):
    split_rows(nn(normed_ref[...], dqkv_ref[0]), buffer, core_ref[0], rows_dev, keep_ref, send_ref)


def qkv_gradients(core, normed_t, dqkv, rows_dev):
    length = normed_t.shape[1]
    half = pl.BlockSpec((D // 2, D), lambda t: (0, t))
    return pl.pallas_call(
        functools.partial(qkv_grad_kernel, rows_dev),
        grid=(3,),
        in_specs=[
            SCALARS, whole_spec((D, length), **ONCE), pl.BlockSpec((1, length, D), lambda t: (t, 0, 0)),
        ],
        out_specs=[half, half],
        out_shape=[jax.ShapeDtypeStruct((D // 2, 3 * D), jnp.bfloat16)] * 2,
        scratch_shapes=[pltpu.VMEM((2, D // 2, D), jnp.float32)],
        compiler_params=params_of(40),
        cost_estimate=SMALL,
        name="qkv_gradients",
    )(core, normed_t, dqkv)


def input_kernel(
    core_ref, tokens_ref, dx_ref, dqkv_ref, own_ref, other_ref, params_ref,
    out_ref, sums_ref, wide,
):
    core = core_ref[0]
    wide[:, :LEAD] = jnp.zeros((T, LEAD), jnp.bfloat16)
    for t in range(3):
        wide[:, LEAD + t * D : LEAD + (t + 1) * D] = dqkv_ref[t]
    place = lambda side: pl.ds(pl.multiple_of(side * HALF, 128), HALF)
    dh = nt(wide[:, place(core)], own_ref[...]) + nt(wide[:, place(1 - core)], other_ref[...])
    xhat, inverse = row_norm(tokens_ref[...].astype(jnp.float32))
    both = row_sums(dh, xhat)
    sums_ref[...] = jnp.where(pl.program_id(0) == 0, both, sums_ref[...] + both)
    out_ref[...] = (dx_ref[...] + norm_backward(dh, xhat, inverse, params_ref[0:1])).astype(jnp.bfloat16)


def input_gradient(core, tokens, dx, dqkv, own, other, params):
    length = tokens.shape[0]
    rows = pl.BlockSpec((T, D), lambda i: (i, 0))
    return pl.pallas_call(
        input_kernel,
        grid=(length // T,),
        in_specs=[
            SCALARS, rows, rows, pl.BlockSpec((3, T, D), lambda i: (0, i, 0)),
            whole_spec((D, HALF), **ONCE), whole_spec((D, HALF), **ONCE), whole_spec((8, D)),
        ],
        out_specs=[rows, whole_spec((2, D))],
        out_shape=[
            jax.ShapeDtypeStruct((length, D), jnp.bfloat16),
            jax.ShapeDtypeStruct((2, D), jnp.float32),
        ],
        scratch_shapes=[pltpu.VMEM((T, EXT), jnp.bfloat16)],
        compiler_params=params_of(32),
        cost_estimate=SMALL,
        name="input_gradient",
    )(core, tokens, dx, dqkv, own, other, params)


def fill_bias(segc_ref, segr_ref, bias, nq, most):
    for i in range(nq):
        for d in range(most+1):
            j=i-most+d
            if j<0: continue
            same = segc_ref[j*T:(j+1)*T,:] == segr_ref[:, i*T:(i+1)*T]
            if j==i:
                kp=lax.broadcasted_iota(jnp.int32,(T,T),0); qp=lax.broadcasted_iota(jnp.int32,(T,T),1)
                same = same & (kp<=qp)
            bias[i, d*T:(d+1)*T, :] = jnp.where(same,0.0,NEG)

def fwd_kernel(first_ref, q_ref,k_ref,v_ref,segc_ref,segr_ref,o_ref,lse_ref,bias,kh,vt,*,nq,most):
    @pl.when(pl.program_id(0)==0)
    def _(): fill_bias(segc_ref,segr_ref,bias,nq,most)
    lane=lax.broadcasted_iota(jnp.int32,(1,2*HD),1)
    kh[0]=jnp.where(lane<HD,k_ref[...],0)
    kh[1]=jnp.where(lane>=HD,k_ref[...],0)
    vt[...]=v_ref[...].T
    for i in range(nq):
        hi=(i+1)*T
        qt=q_ref[i*T:hi,:]*SCALE
        def variant(n):
            lo=hi-n*T
            outs=[]
            for h in range(2):
                s=nt(kh[h,lo:hi,:],qt)+bias[i,(most+1-n)*T:,:]
                top=jnp.max(s,axis=0,keepdims=True)
                e=jnp.exp(s-top)
                tot=jnp.sum(e,axis=0,keepdims=True)
                ot=nn(vt[h*HD:(h+1)*HD,lo:hi],e.astype(jnp.bfloat16))
                outs.append(ot*(1.0/tot))
                lse_ref[0,h:h+1,i*T:hi]=top+jnp.log(tot)
            o_ref[i*T:hi,:]=jnp.concatenate(outs,axis=0).T.astype(jnp.bfloat16)
        for n in range(1,min(i,most)+2):
            pl.when(first_ref[i]==n)(functools.partial(variant,n))

def tiles_needed(seg, nq, most):
    last=seg[T-1::T]; first=seg[0::T]
    j=jnp.arange(nq)
    need=(last[None,:]>=first[:,None])&(j[None,:]<=j[:,None])
    return jnp.sum(need,axis=1).astype(jnp.int32)

def attend_fwd(qkv, seg, most=MOST//T):
    S=qkv.shape[0]; nq=S//T
    most=min(most,nq-1)
    first=tiles_needed(seg,nq,most)
    f=pl.pallas_call(functools.partial(fwd_kernel,nq=nq,most=most),
      grid_spec=pltpu.PrefetchScalarGridSpec(num_scalar_prefetch=1,grid=(H//2,),
       in_specs=[pl.BlockSpec((S,2*HD),lambda h,f:(0,LEAD//128+h)),pl.BlockSpec((S,2*HD),lambda h,f:(0,LEAD//128+H//2+h)),pl.BlockSpec((S,2*HD),lambda h,f:(0,LEAD//128+H+h)),
                 pl.BlockSpec((S,1),lambda h,f:(0,0)),pl.BlockSpec((1,S),lambda h,f:(0,0))],
       out_specs=[pl.BlockSpec((S,2*HD),lambda h,f:(0,h)),pl.BlockSpec((1,2,S),lambda h,f:(h,0,0))],
       scratch_shapes=[pltpu.VMEM((nq,(most+1)*T,T),jnp.float32),pltpu.VMEM((2,S,2*HD),jnp.bfloat16),pltpu.VMEM((2*HD,S),jnp.bfloat16)]),
      out_shape=[jax.ShapeDtypeStruct((S,D),jnp.bfloat16),jax.ShapeDtypeStruct((H//2,2,S),jnp.float32)],
      compiler_params=params_of(48),cost_estimate=SMALL,name="attention_forward")
    return f(first,qkv,qkv,qkv,seg.reshape(S,1),seg.reshape(1,S))

PAIRS = 2
PAIR = 2 * HD


def bwd_kernel(
    first_ref, q_ref, k_ref, v_ref, do_ref, o_ref, lse_ref, segc_ref, segr_ref, g_ref,
    bias, key, key_t, key_grad, value_grad, *, nq, most,
):
    @pl.when(pl.program_id(0) == 0)
    def _():
        fill_bias(segc_ref, segr_ref, bias, nq, most)

    lane = lax.broadcasted_iota(jnp.int32, (1, PAIR), 1)
    mine = (lane < HD, lane >= HD)
    groups = [slice(pair * PAIR, (pair + 1) * PAIR) for pair in range(PAIRS)]
    for pair, lanes in enumerate(groups):
        for h in range(2):
            key[2 * pair + h] = jnp.where(mine[h], k_ref[:, lanes], 0)
    key_t[...] = k_ref[...].T
    key_grad[...] = jnp.zeros_like(key_grad)
    value_grad[...] = jnp.zeros_like(value_grad)
    for i in range(nq):
        rows = slice(i * T, (i + 1) * T)

        def variant(n, i=i, rows=rows):
            keys = slice((i + 1 - n) * T, (i + 1) * T)
            mask = bias[i, (most + 1 - n) * T :, :]
            for pair, lanes in enumerate(groups):
                query = q_ref[rows, lanes] * SCALE
                grad = do_ref[rows, lanes]
                meet = (grad.astype(jnp.float32) * o_ref[rows, lanes].astype(jnp.float32)).T
                outs = []
                for h in range(2):
                    head = 2 * pair + h
                    query_h = jnp.where(mine[h], query, 0)
                    grad_h = jnp.where(mine[h], grad, 0)
                    scores = nt(key[head, keys, :], query) + mask
                    probs = jnp.exp(scores - lse_ref[pair, h : h + 1, rows])
                    prob_grad = nt(v_ref[keys, lanes], grad_h)
                    value_grad[keys, lanes] += nn(probs.astype(jnp.bfloat16), grad_h)
                    delta = jnp.sum(meet[h * HD : (h + 1) * HD], axis=0, keepdims=True)
                    score_grad = (probs * (prob_grad - delta)).astype(jnp.bfloat16)
                    key_grad[keys, lanes] += nn(score_grad, query_h)
                    outs.append(nn(key_t[head * HD : (head + 1) * HD, keys], score_grad))
                total = jnp.concatenate(outs, axis=0) * SCALE
                g_ref[0, rows, lanes] = total.T.astype(jnp.bfloat16)

        for n in range(1, min(i, most) + 2):
            pl.when(first_ref[i] == n)(functools.partial(variant, n))
    g_ref[1] = key_grad[...].astype(jnp.bfloat16)
    g_ref[2] = value_grad[...].astype(jnp.bfloat16)


def attend_bwd(qkv, grad, out, lse, seg):
    length = qkv.shape[0]
    nq = length // T
    most = min(MOST // T, nq - 1)
    wide = PAIRS * PAIR
    steps = D // wide
    first = tiles_needed(seg, nq, most)
    columns = lambda start: pl.BlockSpec((length, wide), lambda h, f: (0, start // wide + h))
    return pl.pallas_call(
        functools.partial(bwd_kernel, nq=nq, most=most),
        grid_spec=pltpu.PrefetchScalarGridSpec(
            num_scalar_prefetch=1,
            grid=(steps,),
            in_specs=[
                columns(LEAD), columns(LEAD + D), columns(LEAD + 2 * D), columns(0), columns(0),
                pl.BlockSpec((PAIRS, 2, length), lambda h, f: (h, 0, 0)),
                whole_spec((length, 1)), whole_spec((1, length)),
            ],
            out_specs=pl.BlockSpec((3, length, wide), lambda h, f: (0, 0, h)),
            scratch_shapes=[
                pltpu.VMEM((nq, (most + 1) * T, T), jnp.float32),
                pltpu.VMEM((2 * PAIRS, length, PAIR), jnp.bfloat16),
                pltpu.VMEM((wide, length), jnp.bfloat16),
                pltpu.VMEM((length, wide), jnp.float32),
                pltpu.VMEM((length, wide), jnp.float32),
            ],
        ),
        out_shape=jax.ShapeDtypeStruct((3, length, D), jnp.bfloat16),
        compiler_params=params_of(),
        cost_estimate=SMALL,
        name="attention_backward",
    )(first, qkv, qkv, qkv, grad, out, lse, seg.reshape(length, 1), seg.reshape(1, length))


def after(value, *others):
    return lax.optimization_barrier((value, *others))[0]


def xor_permute(value, mask, devices):
    return lax.ppermute(value, AXES, [(i, i ^ mask) for i in range(devices)])


def by_coordinate(pieces, coordinate):
    count = len(pieces)
    index = lax.broadcasted_iota(jnp.int32, (count,) + pieces[0].shape, 0) ^ coordinate
    out = pieces[0][None]
    for m in range(1, count):
        out = jnp.where(index == m, pieces[m][None], out)
    return out


def gather_rows(mine, dp, fsdp):
    devices = dp * fsdp
    core, z = lax.axis_index("fsdp") % 2, lax.axis_index("fsdp") // 2
    part = lambda side: lax.dynamic_slice_in_dim(mine, side * HALF, HALF, axis=1)

    def spread(value, unit, count, coordinate):
        pieces = [value] + [xor_permute(value, m * unit, devices) for m in range(1, count)]
        return by_coordinate(pieces, coordinate)

    value = by_coordinate([part(core), xor_permute(part(1 - core), 1, devices)], core)
    value = spread(value, 2, fsdp // 2, z)
    value = spread(value, fsdp, dp, lax.axis_index("dp"))
    own = value.reshape(D, HALF)
    return own, xor_permute(own, 1, devices)


def add_pair(keep, got):
    return (keep.astype(jnp.float32) + got.astype(jnp.float32)).astype(jnp.bfloat16)


def add_planes(value, cover):
    value = lax.all_to_all(value, "dp", split_axis=0, concat_axis=0, tiled=True)
    return jnp.sum(after(value, cover).astype(jnp.float32), axis=0).astype(jnp.bfloat16)


def scatter_planes(value):
    return lax.psum_scatter(value, "dp", scatter_dimension=0, tiled=True)


def scatter_column(value, fsdp):
    groups = [[2 * z + c for z in range(fsdp // 2)] for c in range(2)]
    return lax.psum_scatter(
        value, "fsdp", scatter_dimension=0, axis_index_groups=groups, tiled=True
    )


def add_column(value, devices):
    chips = value.shape[0]
    z = lax.axis_index("fsdp") // 2
    take = lambda index: lax.dynamic_index_in_dim(value, index, 0, keepdims=False)
    total = take(z).astype(jnp.float32)
    for m in range(1, chips):
        total = total + xor_permute(take(z ^ m), 2 * m, devices).astype(jnp.float32)
    return total


def pack_kernel(owners_ref, late_ref, early_ref, grads_ref, out_ref):
    out_ref[...] = jnp.zeros_like(out_ref)
    late = late_ref.shape[1]
    grads_ref[:, :late] = late_ref[...]
    grads_ref[:, late:] = early_ref[...].astype(jnp.float32)
    for block in range(grads_ref.shape[1] // D):
        columns = slice(block * D, (block + 1) * D)
        out_ref[owners_ref[block]] = grads_ref[:, columns].astype(jnp.bfloat16)


def pack_blocks(owners, late, early, devices):
    rows = late.shape[0]
    vmem = pl.BlockSpec(memory_space=pltpu.VMEM)
    return pl.pallas_call(
        pack_kernel,
        in_specs=[SCALARS, vmem, vmem],
        out_specs=[vmem, vmem],
        out_shape=[
            jax.ShapeDtypeStruct((rows, late.shape[1] + early.shape[1]), jnp.float32),
            jax.ShapeDtypeStruct((devices, rows, D), jnp.bfloat16),
        ],
        compiler_params=pltpu.CompilerParams(vmem_limit_bytes=16 * MIB),
        cost_estimate=SMALL,
        name="pack_blocks",
    )(owners, late, early)


def step_kernel(rate_ref, grad_ref, left_ref, right_ref, out_ref):
    half = nn(left_ref[...], grad_ref[...]).astype(jnp.bfloat16)
    precond = nn(half, right_ref[...])
    mean = jnp.sum(jnp.sum(precond * precond, axis=0, keepdims=True), axis=1, keepdims=True) * (
        1.0 / (D * D)
    )
    out_ref[...] = (precond * (rate_ref[0] * lax.rsqrt(mean + 1e-06))).astype(jnp.bfloat16)


def owner_step(rate, grad, left, right):
    vmem = pl.BlockSpec(memory_space=pltpu.VMEM)
    return pl.pallas_call(
        step_kernel,
        in_specs=[pl.BlockSpec(memory_space=pltpu.SMEM), vmem, vmem, vmem],
        out_specs=vmem,
        out_shape=jax.ShapeDtypeStruct((D, D), jnp.bfloat16),
        compiler_params=pltpu.CompilerParams(vmem_limit_bytes=24 * MIB),
        name="owner_step",
    )(rate.reshape(1), grad, left, right)


def update_kernel(owners_ref, step_ref, weight_ref, average_ref, new_ref, mean_ref):
    for block in range(weight_ref.shape[1] // D):
        columns = slice(block * D, (block + 1) * D)
        fresh = weight_ref[:, columns] - step_ref[owners_ref[block]].astype(jnp.float32)
        new_ref[:, columns] = fresh
        mean_ref[:, columns] = 0.9 * average_ref[:, columns] + 0.1 * fresh


def update_weights(owners, steps, weights, average):
    vmem = pl.BlockSpec(memory_space=pltpu.VMEM)
    return pl.pallas_call(
        update_kernel,
        in_specs=[pl.BlockSpec(memory_space=pltpu.SMEM), vmem, vmem, vmem],
        out_specs=[vmem, vmem],
        out_shape=[jax.ShapeDtypeStruct(weights.shape, jnp.float32)] * 2,
        compiler_params=pltpu.CompilerParams(vmem_limit_bytes=16 * MIB),
        name="update_weights",
    )(owners, steps, weights, average)


def block_rates(count):
    index = jnp.arange(count, dtype=jnp.int32)
    fc_end = 4 + FF // D
    small = 0.8 / math.sqrt(D)
    return jnp.where(
        index < 3, small, jnp.where(index == 3, 0.4, jnp.where(index < fc_end, small, 0.2))
    )


def on_device(
    dp,
    fsdp,
    tokens,
    cotangent,
    segments,
    owners,
    matrices,
    average,
    vectors,
    vec_moment,
    left_stats,
    right_stats,
    left_roots,
    right_roots,
):
    devices = dp * fsdp
    rank = lax.axis_index(AXES)
    core = (lax.axis_index("fsdp") % 2).reshape(1)
    rows_dev = matrices.shape[0]
    seg = segments[0]
    x = tokens.reshape(-1, D)
    narrow = matrices.astype(jnp.bfloat16)
    lead = jnp.pad(vectors.astype(jnp.bfloat16).T, ((0, 0), (0, LEAD - 4)))
    own, other = gather_rows(jnp.concatenate([lead, narrow[:, : 3 * D]], axis=1), dp, fsdp)
    rest = lax.all_gather(narrow[:, 3 * D :], AXES, axis=0, tiled=True)
    qkv, normed_t, params = qkv_forward(core, x, own, other)
    mixed, sums = attend_fwd(qkv, seg)
    dy = cotangent.reshape(-1, D)
    pair = lambda value: xor_permute(value, 1, devices)
    residual, active, slope, proj_keep, proj_send = block_forward(
        core, mixed, x, dy, rest, params, rows_dev
    )
    proj = scatter_planes(add_pair(proj_keep, pair(proj_send)))
    dx, do, sums_two, middle_keep, middle_send = block_backward(
        core, mixed, residual, dy, slope, rest, params, rows_dev
    )
    middle = scatter_planes(after(add_pair(middle_keep, pair(middle_send)), proj))
    dqkv = attend_bwd(qkv, do, mixed, sums, seg)
    late_keep, late_send = qkv_gradients(core, normed_t, dqkv, rows_dev)
    late = add_pair(late_keep, pair(late_send)).reshape(dp, fsdp // 2, rows_dev, 3 * D)
    early = jnp.concatenate([after(middle, late), proj], axis=1)
    input_grad, sums_one = input_gradient(core, x, dx, after(dqkv, early), own, other, params)
    early = scatter_column(early, fsdp)
    late = add_planes(late, input_grad)
    late = add_column(late, devices)
    vector_terms = jnp.concatenate([sums_one, sums_two], axis=0)
    vector_terms = vector_terms.reshape(4, devices, -1).swapaxes(0, 1)
    vector_parts = lax.all_to_all(vector_terms, AXES, split_axis=0, concat_axis=0, tiled=True)
    vector_grads = jnp.sum(vector_parts, axis=0)
    late = after(late, vector_grads)
    matrix_grads, outgoing = pack_blocks(owners, late, early, devices)
    bf16 = lambda value: value.astype(jnp.bfloat16)
    left_root, right_root = bf16(after(left_roots[0], outgoing)), bf16(after(right_roots[0], outgoing))
    whole = lax.all_to_all(outgoing, AXES, split_axis=0, concat_axis=0, tiled=True)
    outputs = block_outputs(residual, after(active, outgoing), rest)
    block_grad = after(whole, outputs).reshape(D, D)
    mine = (owners == rank).astype(jnp.float32)
    rate = jnp.sum(mine * block_rates(owners.shape[0]))
    step = owner_step(rate, block_grad, left_root, right_root)
    returned = lax.all_to_all(
        step.reshape(devices, rows_dev, D), AXES, split_axis=0, concat_axis=0, tiled=True
    )
    left_next = 0.5 * left_stats[0] + 0.5 * nt(block_grad, block_grad)
    right_next = 0.5 * right_stats[0] + 0.5 * tn(block_grad, block_grad)
    new_matrices, average_new = update_weights(owners, returned, matrices, average)
    moment_new = 0.5 * vec_moment + 0.5 * vector_grads * vector_grads
    vectors_new = vectors - 0.2 * vector_grads / (jnp.sqrt(moment_new) + 1e-08)
    return (
        outputs.reshape(tokens.shape),
        input_grad.reshape(tokens.shape),
        matrix_grads,
        vector_grads,
        left_next[None],
        right_next[None],
        new_matrices,
        moment_new,
        vectors_new,
        average_new,
    )


def solution(mesh):
    in_specs = (
        P(("dp", "fsdp"), None, None),
        P(("dp", "fsdp"), None, None),
        P(("dp", "fsdp"), None),
        P(),
        P(("dp", "fsdp"), None),
        P(("dp", "fsdp"), None),
        P(None, ("dp", "fsdp")),
        P(None, ("dp", "fsdp")),
        P(("dp", "fsdp"), None, None),
        P(("dp", "fsdp"), None, None),
        P(("dp", "fsdp"), None, None),
        P(("dp", "fsdp"), None, None),
    )
    out_specs = (
        P(("dp", "fsdp"), None, None),
        P(("dp", "fsdp"), None, None),
        P(("dp", "fsdp"), None),
        P(None, ("dp", "fsdp")),
        P(("dp", "fsdp"), None, None),
        P(("dp", "fsdp"), None, None),
        P(("dp", "fsdp"), None),
        P(None, ("dp", "fsdp")),
        P(None, ("dp", "fsdp")),
        P(("dp", "fsdp"), None),
    )
    return jax.shard_map(
        functools.partial(on_device, mesh.shape["dp"], mesh.shape["fsdp"]), mesh=mesh, in_specs=in_specs, out_specs=out_specs, check_vma=False
    )
```

```python
import functools
import math

import jax
import jax.numpy as jnp
from jax import lax
from jax.experimental import pallas as pl
from jax.experimental.pallas import tpu as pltpu
from jax.sharding import PartitionSpec as P

D = 768
H = 12
HD = 64
FF = 3072
BRANCHES = 48
BRANCH = BRANCHES ** (-0.5)
SCALE = HD ** (-0.5)
MOST = 512
T = 256
LEAD = 256
EXT = LEAD + 3 * D
HALF = EXT // 2
CHUNK = 768
NEG = -1e30
GELU_A = math.sqrt(2.0 / math.pi)
GELU_B = 0.044715
AXES = ("dp", "fsdp")
MIB = 1 << 20
SMALL = pl.CostEstimate(flops=1024, bytes_accessed=1024, transcendentals=0)


def nt(a, b):
    return lax.dot_general(a, b, (((1,), (1,)), ((), ())), preferred_element_type=jnp.float32)


def nn(a, b):
    return lax.dot_general(a, b, (((1,), (0,)), ((), ())), preferred_element_type=jnp.float32)


def tn(a, b):
    return lax.dot_general(a, b, (((0,), (0,)), ((), ())), preferred_element_type=jnp.float32)


def row_norm(rows):
    centre = rows - jnp.mean(rows, axis=-1, keepdims=True)
    inverse = lax.rsqrt(jnp.mean(centre * centre, axis=-1, keepdims=True) + 1e-05)
    return centre * inverse, inverse


def norm_backward(gradient, xhat, inverse, gain):
    e = gradient * gain
    return inverse * (
        e - jnp.mean(e, axis=-1, keepdims=True) - xhat * jnp.mean(e * xhat, axis=-1, keepdims=True)
    )


def row_sums(gradient, xhat):
    return jnp.concatenate(
        [jnp.sum(gradient * xhat, axis=0, keepdims=True), jnp.sum(gradient, axis=0, keepdims=True)],
        axis=0,
    )


def whole_spec(shape, **kwargs):
    return pl.BlockSpec(shape, lambda *_: (0,) * len(shape), **kwargs)


ONCE = dict(pipeline_mode=pl.Buffered(1))
SCALARS = pl.BlockSpec(memory_space=pltpu.SMEM)


def params_of(vmem=None):
    return pltpu.CompilerParams(vmem_limit_bytes=60 * MIB)


def qkv_kernel(core_ref, tokens_ref, own_ref, other_ref, qkv_ref, normed_ref, params_ref):
    core = core_ref[0]

    @pl.when(pl.program_id(0) == 0)
    def _():
        lead = jnp.where(core == 0, own_ref[:, :128].astype(jnp.float32), other_ref[:, :128].astype(jnp.float32))
        params_ref[...] = lead.T[:8]

    xhat, _ = row_norm(tokens_ref[...].astype(jnp.float32))
    normed = (xhat * params_ref[0:1] + params_ref[1:2]).astype(jnp.bfloat16)
    normed_ref[...] = normed.T
    for side, weights in ((core, own_ref), (1 - core, other_ref)):
        columns = pl.ds(pl.multiple_of(side * HALF, 128), HALF)
        qkv_ref[:, columns] = nn(normed, weights[...]).astype(jnp.bfloat16)


def qkv_forward(core, tokens, own, other):
    length = tokens.shape[0]
    return pl.pallas_call(
        qkv_kernel,
        grid=(length // T,),
        in_specs=[
            SCALARS,
            pl.BlockSpec((T, D), lambda i: (i, 0)),
            whole_spec((D, HALF), **ONCE),
            whole_spec((D, HALF), **ONCE),
        ],
        out_specs=[
            pl.BlockSpec((T, EXT), lambda i: (i, 0)),
            pl.BlockSpec((D, T), lambda i: (0, i)),
            whole_spec((8, D)),
        ],
        out_shape=[
            jax.ShapeDtypeStruct((length, EXT), jnp.bfloat16),
            jax.ShapeDtypeStruct((D, length), jnp.bfloat16),
            jax.ShapeDtypeStruct((8, D), jnp.float32),
        ],
        compiler_params=params_of(32),
        cost_estimate=SMALL,
        name="qkv_forward",
    )(core, tokens, own, other)


def split_rows(total, buffer, core, rows, keep_ref, send_ref):
    for part in range(total.shape[0] // rows):
        place = part // 2 * rows
        buffer[part % 2, place : place + rows] = total[part * rows : (part + 1) * rows]
    keep_ref[...] = buffer[core].astype(jnp.bfloat16)
    send_ref[...] = buffer[1 - core].astype(jnp.bfloat16)


def forward_kernel(
    rows_dev, core_ref, mixed_ref, tokens_ref, cotangent_ref, out_ref, up_ref, params_ref,
    residual_ref, active_ref, slope_ref, keep_ref, send_ref, normed, incoming, buffer,
):
    step = pl.program_id(0)
    tiles = [slice(start, start + T) for start in range(0, normed.shape[0], T)]

    @pl.when(step == 0)
    def _():
        for rows in tiles:
            residual = (
                tokens_ref[rows].astype(jnp.float32) + nn(mixed_ref[rows], out_ref[...]) * BRANCH
            )
            residual_ref[rows] = residual
            xhat, _ = row_norm(residual)
            normed[rows] = (xhat * params_ref[2:3] + params_ref[3:4]).astype(jnp.bfloat16)
            incoming[:, rows] = (cotangent_ref[rows].astype(jnp.float32) * BRANCH).astype(jnp.bfloat16).T

    for rows in tiles:
        u = nn(normed[rows], up_ref[...])
        square = u * u
        bend = jnp.tanh(u * (GELU_A + (GELU_A * GELU_B) * square))
        half = 0.5 + 0.5 * bend
        product = u * half
        active_ref[rows] = product.astype(jnp.bfloat16)
        slope = half + product * ((1.0 - bend) * (GELU_A + (3.0 * GELU_A * GELU_B) * square))
        slope_ref[rows] = slope.astype(jnp.bfloat16)
    split_rows(nn(incoming[...], active_ref[...]), buffer, core_ref[0], rows_dev, keep_ref, send_ref)


def block_forward(core, mixed, tokens, cotangent, weights, params, rows_dev):
    length = tokens.shape[0]
    parts = FF // D
    whole = whole_spec((length, D), **ONCE)
    weight = lambda first: pl.BlockSpec((D, D), lambda i: (0, first + i))
    half = pl.BlockSpec((D // 2, D), lambda i: (0, i))
    return pl.pallas_call(
        functools.partial(forward_kernel, rows_dev),
        grid=(parts,),
        in_specs=[
            SCALARS, whole, whole, whole, whole_spec((D, D), **ONCE), weight(1),
            whole_spec((8, D)),
        ],
        out_specs=[
            whole_spec((length, D)), pl.BlockSpec((length, D), lambda i: (0, i)),
            pl.BlockSpec((length, D), lambda i: (0, i)), half, half,
        ],
        out_shape=[
            jax.ShapeDtypeStruct((length, D), jnp.float32),
            jax.ShapeDtypeStruct((length, FF), jnp.bfloat16),
            jax.ShapeDtypeStruct((length, FF), jnp.bfloat16),
            jax.ShapeDtypeStruct((D // 2, FF), jnp.bfloat16),
            jax.ShapeDtypeStruct((D // 2, FF), jnp.bfloat16),
        ],
        scratch_shapes=[
            pltpu.VMEM((length, D), jnp.bfloat16),
            pltpu.VMEM((D, length), jnp.bfloat16),
            pltpu.VMEM((2, D // 2, D), jnp.float32),
        ],
        compiler_params=params_of(),
        cost_estimate=SMALL,
        name="block_forward",
    )(core, mixed, tokens, cotangent, weights, weights, params)


def output_kernel(residual_ref, active_ref, *refs):
    total = residual_ref[...]
    for part, down_ref in enumerate(refs[:-1]):
        total += nt(active_ref[:, part * D : (part + 1) * D], down_ref[...]) * BRANCH
    refs[-1][...] = total.astype(jnp.bfloat16)


def block_outputs(residual, active, weights):
    length = residual.shape[0]
    parts = FF // D
    rows = lambda width: pl.BlockSpec((T, width), lambda i: (i, 0))
    down = [
        pl.BlockSpec((D, D), lambda i, part=part: (0, 1 + parts + part), **ONCE) for part in range(parts)
    ]
    return pl.pallas_call(
        output_kernel,
        grid=(length // T,),
        in_specs=[rows(D), rows(FF), *down],
        out_specs=rows(D),
        out_shape=jax.ShapeDtypeStruct((length, D), jnp.bfloat16),
        compiler_params=params_of(),
        cost_estimate=SMALL,
        name="block_outputs",
    )(residual, active, *[weights] * parts)


def backward_kernel(
    rows_dev, core_ref, mixed_ref, residual_ref, cotangent_ref, slope_ref, weights_ref, params_ref,
    dx_ref, do_ref, sums_ref, keep_ref, send_ref, inner, normed_t, mixed_t, outer, buffer,
):
    step = pl.program_id(0)
    tiles = inner.shape[0]
    parts = FF // CHUNK

    @pl.when(step < tiles)
    def _():
        weights = lambda block: weights_ref[:, block * D : (block + 1) * D]
        xhat, inverse = row_norm(residual_ref[...])
        normed_t[step] = (xhat * params_ref[2:3] + params_ref[3:4]).astype(jnp.bfloat16).T
        mixed_t[step] = mixed_ref[...].T
        dy = cotangent_ref[...].astype(jnp.float32)
        scaled = (dy * BRANCH).astype(jnp.bfloat16)
        dh = jnp.zeros((T, D), jnp.float32)
        for chunk in range(parts):
            columns = slice(chunk * CHUNK, (chunk + 1) * CHUNK)
            slope = slope_ref[:, columns].astype(jnp.float32)
            du = (nn(scaled, weights(1 + parts + chunk)) * slope).astype(jnp.bfloat16)
            inner[step, :, columns] = du
            dh += nt(du, weights(1 + chunk))
        both = row_sums(dh, xhat)
        sums_ref[...] = jnp.where(step == 0, both, sums_ref[...] + both)
        dx = dy + norm_backward(dh, xhat, inverse, params_ref[2:3])
        dx_ref[...] = dx
        dz = (dx * BRANCH).astype(jnp.bfloat16)
        outer[step] = dz
        do_ref[...] = nt(dz, weights(0)).astype(jnp.bfloat16)

    def gradient(left, right, columns):
        total = nn(left[0], right[0, :, columns])
        for tile in range(1, tiles):
            total += nn(left[tile], right[tile, :, columns])
        split_rows(total, buffer, core_ref[0], rows_dev, keep_ref, send_ref)

    pl.when(step == tiles)(functools.partial(gradient, mixed_t, outer, slice(0, D)))
    for chunk in range(parts):
        columns = slice(chunk * CHUNK, (chunk + 1) * CHUNK)
        pl.when(step == tiles + 1 + chunk)(functools.partial(gradient, normed_t, inner, columns))


def block_backward(core, mixed, residual, cotangent, slope, weights, params, rows_dev):
    length = residual.shape[0]
    tiles = length // T
    rows = lambda width: pl.BlockSpec((T, width), lambda i: (jnp.minimum(i, tiles - 1), 0))
    half = pl.BlockSpec((D // 2, CHUNK), lambda i: (0, jnp.maximum(i - tiles, 0)))
    return pl.pallas_call(
        functools.partial(backward_kernel, rows_dev),
        grid=(tiles + 1 + FF // CHUNK,),
        in_specs=[
            SCALARS, rows(D), rows(D), rows(D), rows(FF), whole_spec(weights.shape, **ONCE),
            whole_spec((8, D)),
        ],
        out_specs=[rows(D), rows(D), whole_spec((2, D)), half, half],
        out_shape=[
            jax.ShapeDtypeStruct((length, D), jnp.float32),
            jax.ShapeDtypeStruct((length, D), jnp.bfloat16),
            jax.ShapeDtypeStruct((2, D), jnp.float32),
            jax.ShapeDtypeStruct((D // 2, D + FF), jnp.bfloat16),
            jax.ShapeDtypeStruct((D // 2, D + FF), jnp.bfloat16),
        ],
        scratch_shapes=[
            pltpu.VMEM((tiles, T, FF), jnp.bfloat16),
            pltpu.VMEM((tiles, D, T), jnp.bfloat16),
            pltpu.VMEM((tiles, D, T), jnp.bfloat16),
            pltpu.VMEM((tiles, T, D), jnp.bfloat16),
            pltpu.VMEM((2, D // 2, CHUNK), jnp.float32),
        ],
        compiler_params=params_of(52),
        cost_estimate=SMALL,
        name="block_backward",
    )(core, mixed, residual, cotangent, slope, weights, params)


def qkv_grad_kernel(rows_dev, core_ref, normed_ref, dqkv_ref, keep_ref, send_ref, buffer):
    split_rows(nn(normed_ref[...], dqkv_ref[0]), buffer, core_ref[0], rows_dev, keep_ref, send_ref)


def qkv_gradients(core, normed_t, dqkv, rows_dev):
    length = normed_t.shape[1]
    half = pl.BlockSpec((D // 2, D), lambda t: (0, t))
    return pl.pallas_call(
        functools.partial(qkv_grad_kernel, rows_dev),
        grid=(3,),
        in_specs=[
            SCALARS, whole_spec((D, length), **ONCE), pl.BlockSpec((1, length, D), lambda t: (t, 0, 0)),
        ],
        out_specs=[half, half],
        out_shape=[jax.ShapeDtypeStruct((D // 2, 3 * D), jnp.bfloat16)] * 2,
        scratch_shapes=[pltpu.VMEM((2, D // 2, D), jnp.float32)],
        compiler_params=params_of(40),
        cost_estimate=SMALL,
        name="qkv_gradients",
    )(core, normed_t, dqkv)


def input_kernel(
    core_ref, tokens_ref, dx_ref, dqkv_ref, own_ref, other_ref, params_ref,
    out_ref, sums_ref, wide,
):
    core = core_ref[0]
    wide[:, :LEAD] = jnp.zeros((T, LEAD), jnp.bfloat16)
    for t in range(3):
        wide[:, LEAD + t * D : LEAD + (t + 1) * D] = dqkv_ref[t]
    place = lambda side: pl.ds(pl.multiple_of(side * HALF, 128), HALF)
    dh = nt(wide[:, place(core)], own_ref[...]) + nt(wide[:, place(1 - core)], other_ref[...])
    xhat, inverse = row_norm(tokens_ref[...].astype(jnp.float32))
    both = row_sums(dh, xhat)
    sums_ref[...] = jnp.where(pl.program_id(0) == 0, both, sums_ref[...] + both)
    out_ref[...] = (dx_ref[...] + norm_backward(dh, xhat, inverse, params_ref[0:1])).astype(jnp.bfloat16)


def input_gradient(core, tokens, dx, dqkv, own, other, params):
    length = tokens.shape[0]
    rows = pl.BlockSpec((T, D), lambda i: (i, 0))
    return pl.pallas_call(
        input_kernel,
        grid=(length // T,),
        in_specs=[
            SCALARS, rows, rows, pl.BlockSpec((3, T, D), lambda i: (0, i, 0)),
            whole_spec((D, HALF), **ONCE), whole_spec((D, HALF), **ONCE), whole_spec((8, D)),
        ],
        out_specs=[rows, whole_spec((2, D))],
        out_shape=[
            jax.ShapeDtypeStruct((length, D), jnp.bfloat16),
            jax.ShapeDtypeStruct((2, D), jnp.float32),
        ],
        scratch_shapes=[pltpu.VMEM((T, EXT), jnp.bfloat16)],
        compiler_params=params_of(32),
        cost_estimate=SMALL,
        name="input_gradient",
    )(core, tokens, dx, dqkv, own, other, params)


def fill_bias(segc_ref, segr_ref, bias, nq, most):
    for i in range(nq):
        for d in range(most+1):
            j=i-most+d
            if j<0: continue
            same = segc_ref[j*T:(j+1)*T,:] == segr_ref[:, i*T:(i+1)*T]
            if j==i:
                kp=lax.broadcasted_iota(jnp.int32,(T,T),0); qp=lax.broadcasted_iota(jnp.int32,(T,T),1)
                same = same & (kp<=qp)
            bias[i, d*T:(d+1)*T, :] = jnp.where(same,0.0,NEG)

def fwd_kernel(first_ref, q_ref,k_ref,v_ref,segc_ref,segr_ref,o_ref,lse_ref,bias,kh,vt,*,nq,most):
    @pl.when(pl.program_id(0)==0)
    def _(): fill_bias(segc_ref,segr_ref,bias,nq,most)
    lane=lax.broadcasted_iota(jnp.int32,(1,2*HD),1)
    kh[0]=jnp.where(lane<HD,k_ref[...],0)
    kh[1]=jnp.where(lane>=HD,k_ref[...],0)
    vt[...]=v_ref[...].T
    for i in range(nq):
        hi=(i+1)*T
        qt=q_ref[i*T:hi,:]*SCALE
        def variant(n):
            lo=hi-n*T
            outs=[]
            for h in range(2):
                s=nt(kh[h,lo:hi,:],qt)+bias[i,(most+1-n)*T:,:]
                top=jnp.max(s,axis=0,keepdims=True)
                e=jnp.exp(s-top)
                tot=jnp.sum(e,axis=0,keepdims=True)
                ot=nn(vt[h*HD:(h+1)*HD,lo:hi],e.astype(jnp.bfloat16))
                outs.append(ot*(1.0/tot))
                lse_ref[0,h:h+1,i*T:hi]=top+jnp.log(tot)
            o_ref[i*T:hi,:]=jnp.concatenate(outs,axis=0).T.astype(jnp.bfloat16)
        for n in range(1,min(i,most)+2):
            pl.when(first_ref[i]==n)(functools.partial(variant,n))

def tiles_needed(seg, nq, most):
    last=seg[T-1::T]; first=seg[0::T]
    j=jnp.arange(nq)
    need=(last[None,:]>=first[:,None])&(j[None,:]<=j[:,None])
    return jnp.sum(need,axis=1).astype(jnp.int32)

def attend_fwd(qkv, seg, most=MOST//T):
    S=qkv.shape[0]; nq=S//T
    most=min(most,nq-1)
    first=tiles_needed(seg,nq,most)
    f=pl.pallas_call(functools.partial(fwd_kernel,nq=nq,most=most),
      grid_spec=pltpu.PrefetchScalarGridSpec(num_scalar_prefetch=1,grid=(H//2,),
       in_specs=[pl.BlockSpec((S,2*HD),lambda h,f:(0,LEAD//128+h)),pl.BlockSpec((S,2*HD),lambda h,f:(0,LEAD//128+H//2+h)),pl.BlockSpec((S,2*HD),lambda h,f:(0,LEAD//128+H+h)),
                 pl.BlockSpec((S,1),lambda h,f:(0,0)),pl.BlockSpec((1,S),lambda h,f:(0,0))],
       out_specs=[pl.BlockSpec((S,2*HD),lambda h,f:(0,h)),pl.BlockSpec((1,2,S),lambda h,f:(h,0,0))],
       scratch_shapes=[pltpu.VMEM((nq,(most+1)*T,T),jnp.float32),pltpu.VMEM((2,S,2*HD),jnp.bfloat16),pltpu.VMEM((2*HD,S),jnp.bfloat16)]),
      out_shape=[jax.ShapeDtypeStruct((S,D),jnp.bfloat16),jax.ShapeDtypeStruct((H//2,2,S),jnp.float32)],
      compiler_params=params_of(48),cost_estimate=SMALL,name="attention_forward")
    return f(first,qkv,qkv,qkv,seg.reshape(S,1),seg.reshape(1,S))

PAIRS = 2
PAIR = 2 * HD


def bwd_kernel(
    first_ref, q_ref, k_ref, v_ref, do_ref, o_ref, lse_ref, segc_ref, segr_ref, g_ref,
    bias, key, key_t, key_grad, value_grad, *, nq, most,
):
    @pl.when(pl.program_id(0) == 0)
    def _():
        fill_bias(segc_ref, segr_ref, bias, nq, most)

    lane = lax.broadcasted_iota(jnp.int32, (1, PAIR), 1)
    mine = (lane < HD, lane >= HD)
    groups = [slice(pair * PAIR, (pair + 1) * PAIR) for pair in range(PAIRS)]
    for pair, lanes in enumerate(groups):
        for h in range(2):
            key[2 * pair + h] = jnp.where(mine[h], k_ref[:, lanes], 0)
    key_t[...] = k_ref[...].T
    key_grad[...] = jnp.zeros_like(key_grad)
    value_grad[...] = jnp.zeros_like(value_grad)
    for i in range(nq):
        rows = slice(i * T, (i + 1) * T)

        def variant(n, i=i, rows=rows):
            keys = slice((i + 1 - n) * T, (i + 1) * T)
            mask = bias[i, (most + 1 - n) * T :, :]
            for pair, lanes in enumerate(groups):
                query = q_ref[rows, lanes] * SCALE
                grad = do_ref[rows, lanes]
                meet = (grad.astype(jnp.float32) * o_ref[rows, lanes].astype(jnp.float32)).T
                outs = []
                for h in range(2):
                    head = 2 * pair + h
                    query_h = jnp.where(mine[h], query, 0)
                    grad_h = jnp.where(mine[h], grad, 0)
                    scores = nt(key[head, keys, :], query) + mask
                    probs = jnp.exp(scores - lse_ref[pair, h : h + 1, rows])
                    prob_grad = nt(v_ref[keys, lanes], grad_h)
                    value_grad[keys, lanes] += nn(probs.astype(jnp.bfloat16), grad_h)
                    delta = jnp.sum(meet[h * HD : (h + 1) * HD], axis=0, keepdims=True)
                    score_grad = (probs * (prob_grad - delta)).astype(jnp.bfloat16)
                    key_grad[keys, lanes] += nn(score_grad, query_h)
                    outs.append(nn(key_t[head * HD : (head + 1) * HD, keys], score_grad))
                total = jnp.concatenate(outs, axis=0) * SCALE
                g_ref[0, rows, lanes] = total.T.astype(jnp.bfloat16)

        for n in range(1, min(i, most) + 2):
            pl.when(first_ref[i] == n)(functools.partial(variant, n))
    g_ref[1] = key_grad[...].astype(jnp.bfloat16)
    g_ref[2] = value_grad[...].astype(jnp.bfloat16)


def attend_bwd(qkv, grad, out, lse, seg):
    length = qkv.shape[0]
    nq = length // T
    most = min(MOST // T, nq - 1)
    wide = PAIRS * PAIR
    steps = D // wide
    first = tiles_needed(seg, nq, most)
    columns = lambda start: pl.BlockSpec((length, wide), lambda h, f: (0, start // wide + h))
    return pl.pallas_call(
        functools.partial(bwd_kernel, nq=nq, most=most),
        grid_spec=pltpu.PrefetchScalarGridSpec(
            num_scalar_prefetch=1,
            grid=(steps,),
            in_specs=[
                columns(LEAD), columns(LEAD + D), columns(LEAD + 2 * D), columns(0), columns(0),
                pl.BlockSpec((PAIRS, 2, length), lambda h, f: (h, 0, 0)),
                whole_spec((length, 1)), whole_spec((1, length)),
            ],
            out_specs=pl.BlockSpec((3, length, wide), lambda h, f: (0, 0, h)),
            scratch_shapes=[
                pltpu.VMEM((nq, (most + 1) * T, T), jnp.float32),
                pltpu.VMEM((2 * PAIRS, length, PAIR), jnp.bfloat16),
                pltpu.VMEM((wide, length), jnp.bfloat16),
                pltpu.VMEM((length, wide), jnp.float32),
                pltpu.VMEM((length, wide), jnp.float32),
            ],
        ),
        out_shape=jax.ShapeDtypeStruct((3, length, D), jnp.bfloat16),
        compiler_params=params_of(),
        cost_estimate=SMALL,
        name="attention_backward",
    )(first, qkv, qkv, qkv, grad, out, lse, seg.reshape(length, 1), seg.reshape(1, length))


def after(value, *others):
    return lax.optimization_barrier((value, *others))[0]


def xor_permute(value, mask, devices):
    return lax.ppermute(value, AXES, [(i, i ^ mask) for i in range(devices)])


def by_coordinate(pieces, coordinate):
    count = len(pieces)
    index = lax.broadcasted_iota(jnp.int32, (count,) + pieces[0].shape, 0) ^ coordinate
    out = pieces[0][None]
    for m in range(1, count):
        out = jnp.where(index == m, pieces[m][None], out)
    return out


def gather_rows(mine, dp, fsdp):
    devices = dp * fsdp
    core, z = lax.axis_index("fsdp") % 2, lax.axis_index("fsdp") // 2
    part = lambda side: lax.dynamic_slice_in_dim(mine, side * HALF, HALF, axis=1)

    def spread(value, unit, count, coordinate):
        pieces = [value] + [xor_permute(value, m * unit, devices) for m in range(1, count)]
        return by_coordinate(pieces, coordinate)

    value = by_coordinate([part(core), xor_permute(part(1 - core), 1, devices)], core)
    value = spread(value, 2, fsdp // 2, z)
    value = spread(value, fsdp, dp, lax.axis_index("dp"))
    own = value.reshape(D, HALF)
    return own, xor_permute(own, 1, devices)


def add_pair(keep, got):
    return (keep.astype(jnp.float32) + got.astype(jnp.float32)).astype(jnp.bfloat16)


def add_planes(value, cover):
    value = lax.all_to_all(value, "dp", split_axis=0, concat_axis=0, tiled=True)
    return jnp.sum(after(value, cover).astype(jnp.float32), axis=0).astype(jnp.bfloat16)


def scatter_planes(value):
    return lax.psum_scatter(value, "dp", scatter_dimension=0, tiled=True)


def scatter_column(value, fsdp):
    groups = [[2 * z + c for z in range(fsdp // 2)] for c in range(2)]
    return lax.psum_scatter(
        value, "fsdp", scatter_dimension=0, axis_index_groups=groups, tiled=True
    )


def add_column(value, devices):
    chips = value.shape[0]
    z = lax.axis_index("fsdp") // 2
    take = lambda index: lax.dynamic_index_in_dim(value, index, 0, keepdims=False)
    total = take(z).astype(jnp.float32)
    for m in range(1, chips):
        total = total + xor_permute(take(z ^ m), 2 * m, devices).astype(jnp.float32)
    return total


def pack_kernel(owners_ref, late_ref, early_ref, grads_ref, out_ref):
    out_ref[...] = jnp.zeros_like(out_ref)
    late = late_ref.shape[1]
    grads_ref[:, :late] = late_ref[...]
    grads_ref[:, late:] = early_ref[...].astype(jnp.float32)
    for block in range(grads_ref.shape[1] // D):
        columns = slice(block * D, (block + 1) * D)
        out_ref[owners_ref[block]] = grads_ref[:, columns].astype(jnp.bfloat16)


def pack_blocks(owners, late, early, devices):
    rows = late.shape[0]
    vmem = pl.BlockSpec(memory_space=pltpu.VMEM)
    return pl.pallas_call(
        pack_kernel,
        in_specs=[SCALARS, vmem, vmem],
        out_specs=[vmem, vmem],
        out_shape=[
            jax.ShapeDtypeStruct((rows, late.shape[1] + early.shape[1]), jnp.float32),
            jax.ShapeDtypeStruct((devices, rows, D), jnp.bfloat16),
        ],
        compiler_params=pltpu.CompilerParams(vmem_limit_bytes=16 * MIB),
        cost_estimate=SMALL,
        name="pack_blocks",
    )(owners, late, early)


def step_kernel(rate_ref, grad_ref, left_ref, right_ref, out_ref):
    half = nn(left_ref[...], grad_ref[...]).astype(jnp.bfloat16)
    precond = nn(half, right_ref[...])
    mean = jnp.sum(jnp.sum(precond * precond, axis=0, keepdims=True), axis=1, keepdims=True) * (
        1.0 / (D * D)
    )
    out_ref[...] = (precond * (rate_ref[0] * lax.rsqrt(mean + 1e-06))).astype(jnp.bfloat16)


def owner_step(rate, grad, left, right):
    vmem = pl.BlockSpec(memory_space=pltpu.VMEM)
    return pl.pallas_call(
        step_kernel,
        in_specs=[pl.BlockSpec(memory_space=pltpu.SMEM), vmem, vmem, vmem],
        out_specs=vmem,
        out_shape=jax.ShapeDtypeStruct((D, D), jnp.bfloat16),
        compiler_params=pltpu.CompilerParams(vmem_limit_bytes=24 * MIB),
        name="owner_step",
    )(rate.reshape(1), grad, left, right)


def update_kernel(owners_ref, step_ref, weight_ref, average_ref, new_ref, mean_ref):
    for block in range(weight_ref.shape[1] // D):
        columns = slice(block * D, (block + 1) * D)
        fresh = weight_ref[:, columns] - step_ref[owners_ref[block]].astype(jnp.float32)
        new_ref[:, columns] = fresh
        mean_ref[:, columns] = 0.9 * average_ref[:, columns] + 0.1 * fresh


def update_weights(owners, steps, weights, average):
    vmem = pl.BlockSpec(memory_space=pltpu.VMEM)
    return pl.pallas_call(
        update_kernel,
        in_specs=[pl.BlockSpec(memory_space=pltpu.SMEM), vmem, vmem, vmem],
        out_specs=[vmem, vmem],
        out_shape=[jax.ShapeDtypeStruct(weights.shape, jnp.float32)] * 2,
        compiler_params=pltpu.CompilerParams(vmem_limit_bytes=16 * MIB),
        name="update_weights",
    )(owners, steps, weights, average)


def block_rates(count):
    index = jnp.arange(count, dtype=jnp.int32)
    fc_end = 4 + FF // D
    small = 0.8 / math.sqrt(D)
    return jnp.where(
        index < 3, small, jnp.where(index == 3, 0.4, jnp.where(index < fc_end, small, 0.2))
    )


def on_device(
    dp,
    fsdp,
    tokens,
    cotangent,
    segments,
    owners,
    matrices,
    average,
    vectors,
    vec_moment,
    left_stats,
    right_stats,
    left_roots,
    right_roots,
):
    devices = dp * fsdp
    rank = lax.axis_index(AXES)
    core = (lax.axis_index("fsdp") % 2).reshape(1)
    rows_dev = matrices.shape[0]
    seg = segments[0]
    x = tokens.reshape(-1, D)
    narrow = matrices.astype(jnp.bfloat16)
    lead = jnp.pad(vectors.astype(jnp.bfloat16).T, ((0, 0), (0, LEAD - 4)))
    own, other = gather_rows(jnp.concatenate([lead, narrow[:, : 3 * D]], axis=1), dp, fsdp)
    rest = lax.all_gather(narrow[:, 3 * D :], AXES, axis=0, tiled=True)
    qkv, normed_t, params = qkv_forward(core, x, own, other)
    mixed, sums = attend_fwd(qkv, seg)
    dy = cotangent.reshape(-1, D)
    pair = lambda value: xor_permute(value, 1, devices)
    residual, active, slope, proj_keep, proj_send = block_forward(
        core, mixed, x, dy, rest, params, rows_dev
    )
    proj = scatter_planes(add_pair(proj_keep, pair(proj_send)))
    dx, do, sums_two, middle_keep, middle_send = block_backward(
        core, mixed, residual, dy, slope, rest, params, rows_dev
    )
    middle = scatter_planes(after(add_pair(middle_keep, pair(middle_send)), proj))
    dqkv = attend_bwd(qkv, do, mixed, sums, seg)
    late_keep, late_send = qkv_gradients(core, normed_t, dqkv, rows_dev)
    late = add_pair(late_keep, pair(late_send)).reshape(dp, fsdp // 2, rows_dev, 3 * D)
    early = jnp.concatenate([after(middle, late), proj], axis=1)
    input_grad, sums_one = input_gradient(core, x, dx, after(dqkv, late), own, other, params)
    early = scatter_column(early, fsdp)
    late = add_planes(late, input_grad)
    late = add_column(late, devices)
    vector_terms = jnp.concatenate([sums_one, sums_two], axis=0)
    vector_terms = vector_terms.reshape(4, devices, -1).swapaxes(0, 1)
    vector_parts = lax.all_to_all(vector_terms, AXES, split_axis=0, concat_axis=0, tiled=True)
    vector_grads = jnp.sum(vector_parts, axis=0)
    late = after(late, vector_grads)
    matrix_grads, outgoing = pack_blocks(owners, late, early, devices)
    bf16 = lambda value: value.astype(jnp.bfloat16)
    left_root, right_root = bf16(after(left_roots[0], outgoing)), bf16(after(right_roots[0], outgoing))
    whole = lax.all_to_all(outgoing, AXES, split_axis=0, concat_axis=0, tiled=True)
    outputs = block_outputs(residual, after(active, outgoing), rest)
    block_grad = after(whole, outputs).reshape(D, D)
    mine = (owners == rank).astype(jnp.float32)
    rate = jnp.sum(mine * block_rates(owners.shape[0]))
    step = owner_step(rate, block_grad, left_root, right_root)
    returned = lax.all_to_all(
        step.reshape(devices, rows_dev, D), AXES, split_axis=0, concat_axis=0, tiled=True
    )
    left_next = 0.5 * left_stats[0] + 0.5 * nt(block_grad, block_grad)
    right_next = 0.5 * right_stats[0] + 0.5 * tn(block_grad, block_grad)
    new_matrices, average_new = update_weights(owners, returned, matrices, average)
    moment_new = 0.5 * vec_moment + 0.5 * vector_grads * vector_grads
    vectors_new = vectors - 0.2 * vector_grads / (jnp.sqrt(moment_new) + 1e-08)
    return (
        outputs.reshape(tokens.shape),
        input_grad.reshape(tokens.shape),
        matrix_grads,
        vector_grads,
        left_next[None],
        right_next[None],
        new_matrices,
        moment_new,
        vectors_new,
        average_new,
    )


def solution(mesh):
    in_specs = (
        P(("dp", "fsdp"), None, None),
        P(("dp", "fsdp"), None, None),
        P(("dp", "fsdp"), None),
        P(),
        P(("dp", "fsdp"), None),
        P(("dp", "fsdp"), None),
        P(None, ("dp", "fsdp")),
        P(None, ("dp", "fsdp")),
        P(("dp", "fsdp"), None, None),
        P(("dp", "fsdp"), None, None),
        P(("dp", "fsdp"), None, None),
        P(("dp", "fsdp"), None, None),
    )
    out_specs = (
        P(("dp", "fsdp"), None, None),
        P(("dp", "fsdp"), None, None),
        P(("dp", "fsdp"), None),
        P(None, ("dp", "fsdp")),
        P(("dp", "fsdp"), None, None),
        P(("dp", "fsdp"), None, None),
        P(("dp", "fsdp"), None),
        P(None, ("dp", "fsdp")),
        P(None, ("dp", "fsdp")),
        P(("dp", "fsdp"), None),
    )
    return jax.shard_map(
        functools.partial(on_device, mesh.shape["dp"], mesh.shape["fsdp"]), mesh=mesh, in_specs=in_specs, out_specs=out_specs, check_vma=False
    )
```
